256 devices in a mesh: req: 64 (over x, z, core), tp: 4 (over y).
Axes of the slice: x: 4, y: 4, z: 8, core: 2. Of those that a mesh axis runs over, the one named last changes fastest.
Arguments:
- hidden_in: bfloat16 [8192, 2048], P('req', 'tp'), may hold values from -48 to 48
- norm_in_gain: float32 [2048], replicated, may hold values from 0.1 to 1.9
- q_weight: bfloat16 [2048, 2048], P(None, 'tp'), may hold values from -0.125 to 0.125
- k_weight: bfloat16 [2048, 512], P(None, 'tp'), may hold values from -0.125 to 0.125
- v_weight: bfloat16 [2048, 512], P(None, 'tp'), may hold values from -0.125 to 0.125
- q_gain: float32 [128], replicated, may hold values from 0.1 to 1.9
- k_gain: float32 [128], replicated, may hold values from 0.1 to 1.9
- o_weight: bfloat16 [2048, 2048], P('tp'), may hold values from -0.125 to 0.125
- key_pages: bfloat16 [4, 3072, 128, 128], P('tp', 'req'), may hold values from -256 to 256
- value_pages: bfloat16 [4, 3072, 128, 128], P('tp', 'req'), may hold values from -6 to 6
- page_table: int32 [576, 32], P('req'), may hold values from 0 to 47, as said below
- cache_len: int32 [576], P('req'), may hold values from 1 to 4096, as said below
- norm_post_gain: float32 [2048], replicated, may hold values from 0.1 to 1.9
- expert_ids: int32 [8192, 8], P('req'), may hold values from 0 to 127, all different within a row; in each aligned block of 128 rows (0 to 127, 128 to 255, ...) at most 12 rows name the same one
- route_weights: float32 [8192, 8], P('req'), may hold values from 0.02 to 0.25
- gate_weight: bfloat16 [128, 2048, 768], P('req', None, 'tp'), may hold values from -0.125 to 0.125
- up_weight: bfloat16 [128, 2048, 768], P('req', None, 'tp'), may hold values from -0.125 to 0.125
- down_weight: bfloat16 [128, 768, 2048], P('req', 'tp'), may hold values from -0.21875 to 0.21875
Outputs:
- layer_out: bfloat16 [8192, 2048], P('req', 'tp')
The draws below stay inside these ranges and needn't reach their ends.
Inputs may be any that keep to these rules, and one draw needn't show every extreme that they name: `cache_len`: in each group of 9 consecutive requests one request holds 4096 cached tokens and another exactly 256; the others hold at most 256. `page_table`: for request r of group g = r // 9, entry j with j * 128 below cache_len[r] names the page, among group g's 48 pages of the caches, that holds the request's cached tokens j * 128 to j * 128 + 127; these pages are distinct within a group. Other entries name arbitrary pages of the group and are not read; pages that no read entry names hold unused data. `expert_ids`: among the 128 rows of one group no expert is named more than 12 times.
All inputs are finite; a program needn't handle non-finite values.
Results may differ from the reference program's by a relative error of at most 0.006.
Values may be sent and summed in bfloat16 or wider, within the bound.
A program may use at most 128 MiB of HBM per device.

```python
import math
import jax
import jax.numpy as jnp
import numpy as np
from jax import lax

D = 2048
HD = 128
HQ = 16
KVH = 4
FF = 768
TOP = 8
PAGE = 128
MAXPG = 32
SHORT_PG = 2
PRE = 120
TOK_DEV = 128
REQS_DEV = 9
POOL = 48
TOKENS = 8192
REQS = 576
PAGES = 3072
EXPERTS = 128
CAP = 12
N_REQ = 64
N_TP = 4


def draw_hidden_in(key, part):
    key_base, key_col, key_row = jax.random.split(jax.random.fold_in(key, 202), 3)
    column = jnp.arange(D, dtype=jnp.float32) / D
    col_scale = 0.3 * jnp.power(10.0, 0.5 * column + 0.5 * jax.random.uniform(key_col, (D,)))
    row_scale = jnp.power(10.0, jax.random.uniform(key_row, (TOKENS, 1), minval=-0.5, maxval=0.5))
    base_draw = jnp.clip(jax.random.normal(key_base, (TOKENS, D)), -5.0, 5.0)
    return (base_draw * row_scale * col_scale[None, :]).astype(jnp.bfloat16)


def draw_key_pages(key, part):
    key_one = jax.random.fold_in(jax.random.fold_in(key, 303), 0)
    values = 2.5 * jnp.clip(jax.random.normal(key_one, (KVH, PAGES, PAGE, HD)), -6.0, 6.0)
    return values.astype(jnp.bfloat16)


def request_layout(key):
    base_key = jax.random.fold_in(key, 101)
    key_long, key_next, key_exp, key_len, key_perm, key_spare = jax.random.split(base_key, 6)
    groups = REQS // REQS_DEV
    short_cap = SHORT_PG * PAGE
    top_exp = short_cap.bit_length() - 1
    long_pick = jax.random.randint(key_long, (groups, 1), 0, REQS_DEV)
    full_pick = (long_pick + 1 + jax.random.randint(key_next, (groups, 1), 0, REQS_DEV - 1)) % REQS_DEV
    exponent = jax.random.randint(key_exp, (groups, REQS_DEV), 0, top_exp + 1)
    low_len = jnp.left_shift(jnp.ones((groups, REQS_DEV), jnp.int32), exponent)
    extra_len = jax.random.randint(key_len, (groups, REQS_DEV), 0, 1 << 30) % low_len
    short_len = jnp.minimum(low_len + extra_len, short_cap)
    member = jnp.arange(REQS_DEV, dtype=jnp.int32)[None, :]
    lengths = jnp.where(member == long_pick, MAXPG * PAGE, jnp.where(member == full_pick, short_cap, short_len)).astype(jnp.int32)
    pages_used = (lengths + PAGE - 1) // PAGE
    page_begin = jnp.cumsum(pages_used, axis=1) - pages_used
    order_keys = jax.random.randint(key_perm, (groups, POOL), 0, 1 << 20) * POOL + jnp.arange(POOL, dtype=jnp.int32)[None, :]
    pool_order = jnp.argsort(order_keys, axis=1).astype(jnp.int32)
    entry_idx = jnp.arange(MAXPG, dtype=jnp.int32)[None, None, :]
    pool_spot = jnp.minimum(page_begin[:, :, None] + entry_idx, POOL - 1).reshape(groups, REQS_DEV * MAXPG)
    pool_taken = jnp.take_along_axis(pool_order, pool_spot, axis=1).reshape(groups, REQS_DEV, MAXPG)
    spare_page = jax.random.randint(key_spare, (groups, REQS_DEV, MAXPG), 0, POOL)
    table = jnp.where(entry_idx < pages_used[:, :, None], pool_taken, spare_page).astype(jnp.int32)
    return (lengths.reshape(REQS), table.reshape(REQS, MAXPG))


def draw_cache_len(key, part):
    return request_layout(key)[0]


def draw_page_table(key, part):
    return request_layout(key)[1]


def block_levels(own_key, shape, shards, smallest, largest):
    def one(position, parts):
        steps = jax.random.uniform(jax.random.fold_in(jax.random.fold_in(own_key, 6), position), (parts,), jnp.float32, smallest / len(shards), largest / len(shards))
        return jnp.repeat(jnp.exp(steps), shape[position] // parts).reshape((-1,) + (1,) * (len(shape) - position - 1))

    gain = one(*shards[0])
    for cut in shards[1:]:
        gain = gain * one(*cut)
    return gain


def assign_block(own_key, own, number, rows, amount, top, reach, lean):
    order = jax.random.permutation(own_key, amount)
    packed, usual = portions_of(amount, rows * top, reach, lean, True), portions_of(amount, rows * top, reach, lean, False)
    places = jnp.arange(amount)

    def named(sizes, rotation):
        used = int((sizes > 0).sum())
        fixed = max(1, used // 4)
        passed = fixed + (places - fixed + rotation * (used - fixed)) % max(1, amount - fixed)
        return jnp.zeros((amount,), jnp.int32).at[order[jnp.where(places < fixed, places, passed)]].set(jnp.asarray(sizes, jnp.int32))

    sizes = jnp.where(number % 4 == 0, named(packed, number // 4), named(usual, number - number // 4 - 1))
    mixed = jax.random.permutation(jax.random.fold_in(own, 3), amount)
    giver, taker = mixed[0:amount // 2 * 2:2], mixed[1:amount // 2 * 2:2]
    margin = jnp.minimum(sizes[giver] - 1, reach - sizes[taker]) // 2
    margin = jnp.where((giver == order[0]) | (taker == order[0]) | (sizes[taker] == 0), 0, jnp.maximum(margin, 0))
    passed = jax.random.randint(jax.random.fold_in(own, 4), (amount // 2,), 0, 1 << 20) % (margin + 1)
    sizes = sizes.at[giver].add(-passed).at[taker].add(passed)
    members = jnp.searchsorted(jnp.cumsum(sizes), jnp.arange(rows * top), side="right").astype(jnp.int32)
    table = members.reshape(top, rows).T
    table = table[jax.random.permutation(jax.random.fold_in(own, 1), rows)]
    rotation = jax.random.randint(jax.random.fold_in(own, 2), (rows, 1), 0, top)
    return jnp.take_along_axis(table, (jnp.arange(top)[None, :] + rotation) % top, axis=1)


def portions_of(amount, total, bound, slope, full):
    portions = [(1 << 20) // math.isqrt(standing ** slope) + 1 for standing in range(1, amount + 1)]
    largest = bound if full else min(bound, max(-(-total // amount), total * portions[0] // sum(portions)))
    least = 1 if total - largest >= amount - 1 else 0
    counts, spare = [largest] + [least] * (amount - 1), total - largest - least * (amount - 1)
    while spare > 0:
        movable = [i for i in range(1, amount) if counts[i] < largest] or [i for i in range(1, amount) if counts[i] < bound]
        whole, left = sum([portions[i] for i in movable]), spare
        for i in movable:
            more = min(bound - counts[i], max(1, left * portions[i] // whole), spare)
            counts[i] = counts[i] + more
            spare = spare - more
    return np.array(counts)


def normal_values(own_key, shape, deviation, bound, pieces=(), kind=jnp.bfloat16):
    loudness = block_levels(own_key, shape, pieces, -0.22, 0.18) if pieces else 1.0
    result = jax.random.normal(own_key, shape, jnp.float32) * deviation * loudness
    return jnp.minimum(jnp.maximum(result, -bound), bound).astype(kind)


def setup_inputs(seed: int = 0) -> dict:
    splits = jax.random.split(jax.random.key(seed), 19)
    hidden_in = draw_hidden_in(jax.random.fold_in(splits[18], 71), 0)
    norm_in_gain = jnp.clip(1.0 + 0.18 * jax.random.normal(splits[1], (D,), jnp.float32), 0.1, 1.9)
    q_weight = normal_values(splits[2], (D, HQ * HD), D ** -0.5, 0.125, ((1, 4),))
    k_weight = normal_values(splits[3], (D, KVH * HD), D ** -0.5, 0.125, ((1, 4),))
    v_weight = normal_values(splits[4], (D, KVH * HD), D ** -0.5, 0.125, ((1, 4),))
    q_gain = jnp.clip(1.0 + 0.18 * jax.random.normal(splits[5], (HD,), jnp.float32), 0.1, 1.9)
    k_gain = jnp.clip(1.0 + 0.18 * jax.random.normal(splits[6], (HD,), jnp.float32), 0.1, 1.9)
    o_weight = normal_values(splits[7], (HQ * HD, D), (HQ * HD) ** -0.5, 0.125, ((0, 4),))
    key_pages = draw_key_pages(jax.random.fold_in(splits[18], 71), 0)
    value_pages = normal_values(splits[9], (KVH, PAGES, PAGE, HD), 1.0, 6.0, ((0, 4), (1, 64)))
    page_table = draw_page_table(jax.random.fold_in(splits[18], 71), 0)
    cache_len = draw_cache_len(jax.random.fold_in(splits[18], 71), 0)
    norm_post_gain = jnp.clip(1.0 + 0.18 * jax.random.normal(splits[12], (D,), jnp.float32), 0.1, 1.9)
    expert_ids_keys = jax.random.split(jax.random.fold_in(splits[13], 1), TOKENS // TOK_DEV)
    expert_ids_turns = jax.random.permutation(jax.random.fold_in(splits[13], 3), TOKENS // TOK_DEV)
    expert_ids = jax.vmap(lambda own, number: assign_block(jax.random.fold_in(splits[13], 2), own, number, TOK_DEV, EXPERTS, TOP, CAP, 2))(expert_ids_keys, expert_ids_turns).reshape((TOKENS, TOP))
    route_weights = jnp.clip(0.02 + 0.23 * jax.random.uniform(splits[14], (TOKENS, TOP), jnp.float32) ** block_levels(splits[14], (TOKENS, TOP), ((0, 64),), -0.2, 0.2), 0.02, 0.25)
    gate_weight = normal_values(splits[15], (EXPERTS, D, FF), D ** -0.5, 0.125, ((0, 64), (2, 4)))
    up_weight = normal_values(splits[16], (EXPERTS, D, FF), D ** -0.5, 0.125, ((0, 64), (2, 4)))
    down_weight = normal_values(splits[17], (EXPERTS, FF, D), FF ** -0.5, 0.21875, ((0, 64), (1, 4)))
    return dict(hidden_in=hidden_in, norm_in_gain=norm_in_gain, q_weight=q_weight, k_weight=k_weight, v_weight=v_weight, q_gain=q_gain, k_gain=k_gain, o_weight=o_weight, key_pages=key_pages, value_pages=value_pages, page_table=page_table, cache_len=cache_len, norm_post_gain=norm_post_gain, expert_ids=expert_ids, route_weights=route_weights, gate_weight=gate_weight, up_weight=up_weight, down_weight=down_weight)


NORM_EPS = 1e-06
ROPE_BASE = 1000000.0

def rms_scale(values, gain_vec):
    mean_square = lax.optimization_barrier(jnp.mean(values * values, axis=-1, keepdims=True))
    return values * lax.rsqrt(mean_square + NORM_EPS) * gain_vec

def rotate(values, positions):
    half_dim = values.shape[-1] // 2
    exponent = jnp.arange(half_dim, dtype=jnp.float32) * (2.0 / values.shape[-1])
    frequency = jnp.power(jnp.float32(ROPE_BASE), -exponent)
    angles = positions.astype(jnp.float32)[:, None] * frequency[None, :]
    cosine = jnp.cos(angles)[:, None, :]
    sine_val = jnp.sin(angles)[:, None, :]
    front_half = values[..., :half_dim]
    back_half = values[..., half_dim:]
    return jnp.concatenate([front_half * cosine - back_half * sine_val, back_half * cosine + front_half * sine_val], axis=-1)

def token_layout(lengths):
    local_idx = jnp.arange(TOK_DEV, dtype=jnp.int32)
    requests = jnp.where(local_idx < PRE, 0, local_idx - PRE + 1).astype(jnp.int32)
    offsets = jnp.where(local_idx < PRE, local_idx, 0).astype(jnp.int32)
    request_hot = (requests[:, None] == jnp.arange(REQS_DEV, dtype=jnp.int32)[None, :]).astype(jnp.int32)
    positions = lax.optimization_barrier(jnp.sum(request_hot * lengths[None, :], axis=1)) + offsets
    return (requests, positions)

def page_slots(table, lengths):
    pages_used = (lengths + PAGE - 1) // PAGE
    entry_live = jnp.arange(MAXPG, dtype=jnp.int32)[None, :] < pages_used[:, None]
    page_match = ((table[:, :, None] == jnp.arange(POOL, dtype=jnp.int32)[None, None, :]) & entry_live[:, :, None]).astype(jnp.int32)
    page_owner = lax.optimization_barrier(jnp.sum(page_match * jnp.arange(REQS_DEV, dtype=jnp.int32)[:, None, None], axis=(0, 1)))
    page_start = lax.optimization_barrier(jnp.sum(page_match * (jnp.arange(MAXPG, dtype=jnp.int32) * PAGE)[None, :, None], axis=(0, 1)))
    page_used = lax.optimization_barrier(jnp.sum(page_match, axis=(0, 1))) > 0
    owner_length = lax.optimization_barrier(jnp.sum(page_match * lengths[:, None, None], axis=(0, 1)))
    slot_pos = page_start[:, None] + jnp.arange(PAGE, dtype=jnp.int32)[None, :]
    slot_live = page_used[:, None] & (slot_pos < owner_length[:, None])
    slot_owner = jnp.where(slot_live, page_owner[:, None], -1).astype(jnp.int32)
    return slot_owner.reshape(POOL * PAGE)

def attend(queries, keys_new, values_new, keys_cache, values_cache, requests, positions, slot_owner):
    inv_root = 1.0 / math.sqrt(queries.shape[-1])
    cache_mask = slot_owner[None, :] == requests[:, None]
    new_mask = (requests[None, :] == requests[:, None]) & (positions[None, :] <= positions[:, None])
    score_cache = jnp.einsum('tkgh,knh->kgtn', queries.astype(jnp.float32), keys_cache.astype(jnp.float32)) * inv_root
    score_new = jnp.einsum('tkgh,skh->kgts', queries.astype(jnp.float32), keys_new.astype(jnp.float32)) * inv_root
    score_cache = jnp.where(cache_mask[None, None], score_cache, -1e+30)
    score_new = jnp.where(new_mask[None, None], score_new, -1e+30)
    row_max = jnp.maximum(lax.optimization_barrier(jnp.max(score_cache, axis=-1, keepdims=True)), lax.optimization_barrier(jnp.max(score_new, axis=-1, keepdims=True)))
    exp_cache = jnp.where(cache_mask[None, None], jnp.exp(score_cache - row_max), 0.0)
    exp_new = jnp.where(new_mask[None, None], jnp.exp(score_new - row_max), 0.0)
    total = lax.optimization_barrier(jnp.sum(exp_cache, axis=-1, keepdims=True)) + lax.optimization_barrier(jnp.sum(exp_new, axis=-1, keepdims=True))
    prob_cache = (exp_cache / total).astype(jnp.bfloat16)
    prob_new = (exp_new / total).astype(jnp.bfloat16)
    mixed = jnp.einsum('kgtn,knh->tkgh', prob_cache.astype(jnp.float32), values_cache.astype(jnp.float32))
    mixed = mixed + jnp.einsum('kgts,skh->tkgh', prob_new.astype(jnp.float32), values_new.astype(jnp.float32))
    return mixed.astype(jnp.bfloat16).reshape(queries.shape[0], -1)

def reference(hidden_in, norm_in_gain, q_weight, k_weight, v_weight, q_gain, k_gain, o_weight, key_pages, value_pages, page_table, cache_len, norm_post_gain, expert_ids, route_weights, gate_weight, up_weight, down_weight):
    group_size = HQ // KVH
    x_float = hidden_in.astype(jnp.float32)
    normed_in = rms_scale(x_float, norm_in_gain).astype(jnp.bfloat16)
    query_lin = jnp.dot(normed_in, q_weight, preferred_element_type=jnp.float32).reshape(TOKENS, HQ, HD)
    key_lin = jnp.dot(normed_in, k_weight, preferred_element_type=jnp.float32).reshape(TOKENS, KVH, HD)
    values_new = jnp.dot(normed_in, v_weight, preferred_element_type=jnp.float32).astype(jnp.bfloat16).reshape(TOKENS, KVH, HD)
    lengths_grp = cache_len.reshape(N_REQ, REQS_DEV)
    table_grp = page_table.reshape(N_REQ, REQS_DEV, MAXPG)

    def group_positions(group_len):
        return token_layout(group_len)[1]
    positions = jax.vmap(group_positions)(lengths_grp).reshape(TOKENS)
    queries = rotate(rms_scale(query_lin, q_gain), positions).astype(jnp.bfloat16)
    keys_new = rotate(rms_scale(key_lin, k_gain), positions).astype(jnp.bfloat16)
    queries_grp = queries.reshape(N_REQ, TOK_DEV, KVH, group_size, HD)
    keys_grp = keys_new.reshape(N_REQ, TOK_DEV, KVH, HD)
    values_grp = values_new.reshape(N_REQ, TOK_DEV, KVH, HD)

    def one_group(inputs):
        group_idx, group_q, group_k, group_v, group_table, group_len = inputs
        requests, group_pos = token_layout(group_len)
        slot_owner = page_slots(group_table, group_len)
        start_page = (group_idx * POOL).astype(jnp.int32)
        keys_cache = lax.dynamic_slice_in_dim(key_pages, start_page, POOL, 1).reshape(KVH, POOL * PAGE, HD)
        values_cache = lax.dynamic_slice_in_dim(value_pages, start_page, POOL, 1).reshape(KVH, POOL * PAGE, HD)
        return attend(group_q, group_k, group_v, keys_cache, values_cache, requests, group_pos, slot_owner)
    attended = lax.map(one_group, (jnp.arange(N_REQ, dtype=jnp.int32), queries_grp, keys_grp, values_grp, table_grp, lengths_grp))
    attended = attended.reshape(TOKENS, HQ * HD)
    residual = x_float + jnp.dot(attended, o_weight, preferred_element_type=jnp.float32)
    normed_post = rms_scale(residual, norm_post_gain).astype(jnp.bfloat16)
    flat_expert = expert_ids.reshape(N_REQ, TOK_DEV * TOP)
    one_hot = (flat_expert[:, :, None] == jnp.arange(EXPERTS, dtype=jnp.int32)[None, None, :]).astype(jnp.int32)
    slot_rank = lax.optimization_barrier(jnp.sum((jnp.cumsum(one_hot, axis=1) - one_hot) * one_hot, axis=2))
    slot_index = flat_expert * (N_REQ * CAP) + jnp.arange(N_REQ, dtype=jnp.int32)[:, None] * CAP + slot_rank
    slot_index = slot_index.reshape(TOKENS * TOP).astype(jnp.int32)
    token_of = jnp.arange(TOKENS * TOP, dtype=jnp.int32) // TOP
    slot_token = jnp.full((EXPERTS * N_REQ * CAP,), TOKENS, jnp.int32).at[slot_index].set(token_of)
    slot_weight = jnp.zeros((EXPERTS * N_REQ * CAP,), jnp.float32).at[slot_index].set(route_weights.reshape(TOKENS * TOP))
    normed_pad = jnp.concatenate([normed_post, jnp.zeros((1, D), jnp.bfloat16)], axis=0)

    def one_expert(carry_sum, inputs):
        token_ids, weights, w_gate, w_up, w_down = inputs
        token_rows = normed_pad[token_ids]
        gate_acts = jnp.dot(token_rows, w_gate, preferred_element_type=jnp.float32)
        up_acts = jnp.dot(token_rows, w_up, preferred_element_type=jnp.float32)
        hidden_act = (jax.nn.silu(gate_acts) * up_acts).astype(jnp.bfloat16)
        part_sums = jnp.einsum('rgf,gfd->rgd', hidden_act.reshape(-1, N_TP, FF // N_TP).astype(jnp.float32), w_down.reshape(N_TP, FF // N_TP, D).astype(jnp.float32)).astype(jnp.bfloat16)
        contrib = lax.optimization_barrier(jnp.sum(part_sums.astype(jnp.float32), axis=1)) * weights[:, None]
        return (carry_sum.at[token_ids].add(contrib), None)
    start_sum = jnp.zeros((TOKENS + 1, D), jnp.float32)
    moe, _ = lax.scan(one_expert, start_sum, (slot_token.reshape(EXPERTS, N_REQ * CAP), slot_weight.reshape(EXPERTS, N_REQ * CAP), gate_weight, up_weight, down_weight))
    return (residual + moe[:TOKENS]).astype(jnp.bfloat16)
```

```python
import functools
import math

import jax
import jax.numpy as jnp
import numpy as np
from jax import lax
from jax.experimental import pallas as pl
from jax.experimental.pallas import tpu as pltpu
from jax.sharding import PartitionSpec as P

PAGE = 128
MAXPG = 32
PRE = 120
TOK = 128
REQS_DEV = 9
POOL = 48
CAP = 12
NORM_EPS = 1e-06
ROPE_BASE = 1000000.0

MESH = pl.DeviceIdType.MESH
F32 = jnp.float32
BF16 = jnp.bfloat16
BLK = 48
CHUNK = 512


def token_layout(lengths):
    local_idx = jnp.arange(TOK, dtype=jnp.int32)
    requests = jnp.where(local_idx < PRE, 0, local_idx - PRE + 1)
    offsets = jnp.where(local_idx < PRE, local_idx, 0)
    request_hot = (requests[:, None] == jnp.arange(REQS_DEV, dtype=jnp.int32)[None, :]).astype(
        jnp.int32
    )
    return jnp.sum(request_hot * lengths[None, :], axis=1) + offsets


def page_slots(table, lengths):
    pages_used = (lengths + PAGE - 1) // PAGE
    entry_live = jnp.arange(MAXPG, dtype=jnp.int32)[None, :] < pages_used[:, None]
    page_match = (
        (table[:, :, None] == jnp.arange(POOL, dtype=jnp.int32)[None, None, :])
        & entry_live[:, :, None]
    ).astype(jnp.int32)
    page_owner = jnp.sum(
        page_match * jnp.arange(REQS_DEV, dtype=jnp.int32)[:, None, None], axis=(0, 1)
    )
    page_start = jnp.sum(
        page_match * (jnp.arange(MAXPG, dtype=jnp.int32) * PAGE)[None, :, None], axis=(0, 1)
    )
    page_used = jnp.sum(page_match, axis=(0, 1)) > 0
    owner_length = jnp.sum(page_match * lengths[:, None, None], axis=(0, 1))
    slot_pos = page_start[:, None] + jnp.arange(PAGE, dtype=jnp.int32)[None, :]
    slot_live = page_used[:, None] & (slot_pos < owner_length[:, None])
    return jnp.where(slot_live, page_owner[:, None], -1)


def rope_tables(positions, head_dim):
    half = head_dim // 2
    exponent = jnp.arange(half, dtype=F32) * (2.0 / head_dim)
    frequency = jnp.power(F32(ROPE_BASE), -exponent)
    angles = positions.astype(F32)[:, None] * frequency[None, :]
    cosine, sine = jnp.cos(angles), jnp.sin(angles)
    return (
        jnp.concatenate([cosine, cosine], axis=1),
        jnp.concatenate([-sine, sine], axis=1),
    )


def mm(a, b):
    return jnp.dot(a, b, preferred_element_type=F32)


def mm_t(a, b):
    return lax.dot_general(a, b, (((1,), (1,)), ((), ())), preferred_element_type=F32)


def iota(shape, dim):
    return lax.broadcasted_iota(jnp.int32, shape, dim)


def layer_kernel(
    nx, nz,
    hid, gin, qgain, kgain, gpost, cos_t, sin_t, owner, ids_t, ids, rw,
    exp_t, slot_t, exp_r, slot_r, perm1, perm2,
    qw, kw, vw, ow, kp, vp, wg_in, wu_in, wd_in,
    out,
    xbuf, nbuf, qw_v, kw_v, vw_v, ow_v, kc, vc, q2, kn, vn, abuf,
    rs_send, rs_recv, st_send, st_recv, nb, resid, s_mat, w_hi, w_lo,
    send1, recv1, zbuf, xe, wg, wu, wd, ye, send2, recv2,
    loc_s, ag_s, ag_r, rs_s, rs_r, st_s, st_r, d1_s, d1_r, d2_s, d2_r, w_s, w_r, f_s,
):
    me_r = lax.axis_index("req")
    my = lax.axis_index("tp")
    core = lax.rem(me_r, 2)
    chip = me_r // 2
    cx = chip // nz
    cz = lax.rem(chip, nz)
    world = chip * 4 + my
    n_world = nx * nz * 4
    n_rows = n_world * CAP
    src_slot = cz * nx + cx

    def peer(k):
        return lax.rem(my + k, 4)

    barrier = pltpu.get_barrier_semaphore()

    def greet(k, carry):
        other = lax.rem(world + k, n_world)
        pl.semaphore_signal(
            barrier, inc=1,
            device_id={"req": (other // 4) * 2 + core, "tp": lax.rem(other, 4)},
            device_id_type=MESH,
        )
        return carry

    lax.fori_loop(1, n_world, greet, 0)
    sibling = {"req": chip * 2 + 1 - core, "tp": my}
    pl.semaphore_signal(barrier, inc=1, device_id=sibling, device_id_type=MESH)

    loads = [
        pltpu.make_async_copy(s, d, loc_s.at[i])
        for i, (s, d) in enumerate(
            [(qw, qw_v), (kw, kw_v), (vw, vw_v), (kp, kc), (vp, vc), (ow, ow_v)]
        )
    ]
    for load in loads:
        load.start()
    xbuf[my] = hid[...]

    lane = iota((TOK, TOK), 1)
    sub = iota((TOK, TOK), 0)
    named_t = jnp.zeros((TOK, TOK), F32)
    named = jnp.zeros((TOK, TOK), F32)
    dense_w = jnp.zeros((TOK, TOK), F32)
    for k in range(8):
        named_t = named_t + (ids_t[k : k + 1, :] == sub).astype(F32)
        hit = (ids[:, k : k + 1] == lane).astype(F32)
        named = named + hit
        dense_w = dense_w + hit * rw[:, k : k + 1]
    before = (sub < lane).astype(BF16)
    after = (lane < sub).astype(BF16)
    rank_t = jnp.where(named_t > 0, mm(named_t.astype(BF16), before), -1.0)
    rank = jnp.where(named > 0, mm(after, named.astype(BF16)), -1.0)
    s_mat[...] = (mm(exp_t[...], rank_t.astype(BF16)) == slot_t[...].astype(F32)).astype(BF16)
    chosen = mm(rank.astype(BF16), exp_r[...]) == slot_r[...]
    dw_hi = dense_w.astype(BF16)
    dw_lo = (dense_w - dw_hi.astype(F32)).astype(BF16)
    w_hi[...] = jnp.where(chosen, mm(dw_hi, exp_r[...]), 0.0).astype(BF16)
    w_lo[...] = jnp.where(chosen, mm(dw_lo, exp_r[...]), 0.0).astype(BF16)

    pl.semaphore_wait(barrier, n_world)

    def ag_copy(k):
        return pltpu.make_async_remote_copy(
            src_ref=hid, dst_ref=xbuf.at[my], send_sem=ag_s.at[k - 1], recv_sem=ag_r.at[k - 1],
            device_id={"tp": peer(k)}, device_id_type=MESH,
        )

    for k in (1, 3, 2):
        ag_copy(k).start()

    w_pairs = ((wg_in, wg), (wu_in, wu), (wd_in, wd))

    def w_remote(a, i):
        return pltpu.make_async_remote_copy(
            src_ref=w_pairs[a][0].at[i], dst_ref=w_pairs[a][1].at[my],
            send_sem=w_s.at[a, i], recv_sem=w_r.at[a, my],
            device_id={"tp": 2 * core + i}, device_id_type=MESH,
        )

    def w_start(a):
        for i in range(2):
            @pl.when(2 * core + i != my)
            def _():
                w_remote(a, i).start()

            @pl.when(2 * core + i == my)
            def _():
                pltpu.make_async_copy(
                    w_pairs[a][0].at[i], w_pairs[a][1].at[my], w_r.at[a, my]
                ).start()

    def w_forward(a, j):
        return pltpu.make_async_remote_copy(
            src_ref=w_pairs[a][1].at[j], dst_ref=w_pairs[a][1].at[j],
            send_sem=f_s.at[a, j], recv_sem=w_r.at[a, j],
            device_id=sibling, device_id_type=MESH,
        )

    def w_wait(a, j):
        ref = w_pairs[a][1].at[j]
        pltpu.make_async_copy(ref, ref, w_r.at[a, j]).wait()

    primary = core == my // 2

    def w_pass_on(a):
        @pl.when(primary)
        def _():
            for j in range(4):
                w_wait(a, j)
                w_forward(a, j).start()

    w_start(0)

    for k in (1, 3, 2):
        ag_copy(k).wait_recv()
    x_all = jnp.concatenate([xbuf[j].astype(F32) for j in range(4)], axis=1)
    mean_sq = jnp.mean(x_all * x_all, axis=-1, keepdims=True)
    nbuf[...] = (x_all * lax.rsqrt(mean_sq + NORM_EPS) * gin[...]).astype(BF16)
    for load in loads[:3]:
        load.wait()

    def head_norm(v, gain):
        ms = jnp.mean(v * v, axis=-1, keepdims=True)
        v = v * lax.rsqrt(ms + NORM_EPS) * gain
        return (v * cos_t[...] + pltpu.roll(v, 64, 1) * sin_t[...]).astype(BF16)

    q_lin = mm(nbuf[...], qw_v[...])
    for g in range(4):
        q2[g * TOK : (g + 1) * TOK, :] = head_norm(q_lin[:, g * 128 : (g + 1) * 128], qgain[...])
    kn[...] = head_norm(mm(nbuf[...], kw_v[...]), kgain[...])
    vn[...] = mm(nbuf[...], vw_v[...]).astype(BF16)

    inv_root = 1.0 / math.sqrt(128)
    n_q = 4 * TOK
    row_tok = lax.rem(iota((n_q, 1), 0), TOK)
    row_req = jnp.where(row_tok < PRE, 0, row_tok - PRE + 1)
    key_tok = iota((n_q, TOK), 1)
    new_mask = (key_tok == row_tok) | ((row_tok < PRE) & (key_tok <= row_tok))
    sc = jnp.where(new_mask, mm_t(q2[...], kn[...]) * inv_root, -1e30)
    m0 = jnp.max(sc, axis=-1, keepdims=True)
    pr = jnp.exp(sc - m0)
    l0 = jnp.sum(pr, axis=-1, keepdims=True)
    acc0 = mm(pr.astype(BF16), vn[...])
    for load in loads[3:5]:
        load.wait()

    def attend_chunk(j, carry):
        m, l, acc = carry
        at = pl.multiple_of(j * CHUNK, CHUNK)
        s = mm_t(q2[...], kc[pl.ds(at, CHUNK), :]) * inv_root
        s = jnp.where(owner[j] == row_req, s, -1e30)
        m_new = jnp.maximum(m, jnp.max(s, axis=-1, keepdims=True))
        scale = jnp.exp(m - m_new)
        p = jnp.exp(s - m_new)
        l = l * scale + jnp.sum(p, axis=-1, keepdims=True)
        acc = acc * scale + mm(p.astype(BF16), vc[pl.ds(at, CHUNK), :])
        return m_new, l, acc

    _, l_all, acc_all = lax.fori_loop(0, POOL * PAGE // CHUNK, attend_chunk, (m0, l0, acc0))
    att = (acc_all / l_all).astype(BF16)
    for g in range(4):
        abuf[:, g * 128 : (g + 1) * 128] = att[g * TOK : (g + 1) * TOK, :]
    loads[5].wait()
    for j in range(4):
        rs_send[j] = mm(abuf[...], ow_v[:, j * 512 : (j + 1) * 512]).astype(BF16)

    def rs_copy(k):
        return pltpu.make_async_remote_copy(
            src_ref=rs_send.at[peer(k)], dst_ref=rs_recv.at[k - 1],
            send_sem=rs_s.at[k - 1], recv_sem=rs_r.at[k - 1],
            device_id={"tp": peer(k)}, device_id_type=MESH,
        )

    for k in (1, 3, 2):
        rs_copy(k).start()
    total = hid[...].astype(F32) + rs_send[my].astype(F32)
    for k in (1, 3, 2):
        rs_copy(k).wait_recv()
        total = total + rs_recv[k - 1].astype(F32)
    resid[...] = total
    col = jnp.sum(total * total, axis=-1, keepdims=True)
    diag = sub == lane
    row = jnp.sum(jnp.where(diag, col, 0.0), axis=0, keepdims=True)
    st_send[...] = jnp.broadcast_to(row, (8, TOK))

    def st_copy(k):
        return pltpu.make_async_remote_copy(
            src_ref=st_send, dst_ref=st_recv.at[k - 1],
            send_sem=st_s.at[k - 1], recv_sem=st_r.at[k - 1],
            device_id={"tp": peer(k)}, device_id_type=MESH,
        )

    for k in (1, 3, 2):
        st_copy(k).start()
    w_start(1)
    w_start(2)
    for k in (1, 3, 2):
        st_copy(k).wait_recv()
    row = st_send[0:1, :] + st_recv[0, 0:1, :] + st_recv[1, 0:1, :] + st_recv[2, 0:1, :]
    col = jnp.sum(jnp.where(diag, row, 0.0), axis=-1, keepdims=True)
    nb[...] = (
        resid[...] * lax.rsqrt(col * (1.0 / 2048.0) + NORM_EPS) * gpost[my]
    ).astype(BF16)

    def dz_of(jj):
        return lax.rem(nz // 2 + ((jj + 1) // 2) * (1 - 2 * lax.rem(jj, 2)) + nz, nz)

    def chip_at(jj, dx):
        return lax.rem(cx + dx, nx), lax.rem(cz + dz_of(jj), nz)

    def d1_copy(jj, dx, k, local=False):
        gx, gz = chip_at(jj, dx)
        g = gx * nz + gz
        src = send1.at[pl.ds(pl.multiple_of((g * 4 + peer(k)) * BLK, 16), BLK)]
        dst = recv1.at[my, pl.ds(pl.multiple_of(src_slot * BLK, 16), BLK)]
        if local:
            return pltpu.make_async_copy(src, dst, d1_r.at[jj])
        return pltpu.make_async_remote_copy(
            src_ref=src, dst_ref=dst, send_sem=d1_s, recv_sem=d1_r.at[jj],
            device_id={"req": g * 2 + core, "tp": peer(k)}, device_id_type=MESH,
        )

    def d2_copy(jj, dx, k, local=False):
        gx, gz = chip_at(jj, dx)
        src = send2.at[peer(k), pl.ds(pl.multiple_of((gz * nx + gx) * BLK, 16), BLK)]
        dst = recv2.at[pl.ds(pl.multiple_of(world * BLK, 16), BLK)]
        if local:
            return pltpu.make_async_copy(src, dst, d2_r.at[jj])
        return pltpu.make_async_remote_copy(
            src_ref=src, dst_ref=dst, send_sem=d2_s, recv_sem=d2_r.at[jj],
            device_id={"req": (gx * nz + gz) * 2 + core, "tp": peer(k)}, device_id_type=MESH,
        )

    def send_all(copy_of, jj, last=False):
        for dx in range(nx):
            for k in range(4):
                copy_of(jj, dx, k, local=last and dx == 0 and k == 0).start()

    def build(jj):
        parts = []
        for dx in range(nx):
            gx, gz = chip_at(jj, dx)
            at = pl.multiple_of((gx * nz + gz) * BLK, 16)
            z = mm(s_mat[pl.ds(at, BLK), :], nb[...]).astype(BF16)
            parts.append(jnp.concatenate([z[:, i * 128 : (i + 1) * 128] for i in range(4)], axis=0))
        o = mm(perm2[...], jnp.concatenate(parts, axis=1)).astype(BF16)
        for dx in range(nx):
            gx, gz = chip_at(jj, dx)
            at = pl.multiple_of((gx * nz + gz) * 4 * BLK, 16)
            send1[pl.ds(at, 4 * BLK), :] = o[:, dx * 128 : (dx + 1) * 128]

    build(0)

    def build_step(jj, carry):
        build(jj)
        send_all(d1_copy, jj - 1)
        return carry

    lax.fori_loop(1, nz, build_step, 0)
    send_all(d1_copy, nz - 1, last=True)

    w_pass_on(0)
    w_pass_on(1)
    w_pass_on(2)

    def d_wait(ref, sem):
        pltpu.make_async_copy(ref, ref, sem).wait()

    for jj in range(nz):
        d_wait(recv1.at[0, pl.ds(0, 4 * nx * BLK)], d1_r.at[jj])

    def unpack(gz, carry):
        at = pl.multiple_of(gz * nx * BLK, 16)
        x = jnp.concatenate([recv1[q, pl.ds(at, nx * BLK), :] for q in range(4)], axis=1)
        o = mm(perm1[...], x).astype(BF16)
        to = pl.multiple_of(gz * BLK, 16)
        for q in range(4):
            for i in range(4):
                xe[pl.ds(to, BLK), (q * 4 + i) * 128 : (q * 4 + i + 1) * 128] = o[
                    i * BLK : (i + 1) * BLK, q * 128 : (q + 1) * 128
                ]
        return carry

    lax.fori_loop(0, nz, unpack, 0)

    @pl.when(jnp.logical_not(primary))
    def _():
        for a in range(3):
            for j in range(4):
                w_wait(a, j)

    half_rows = nx * nz * CAP // 2
    ye[...] = jnp.zeros_like(ye)

    def expert_step(t, carry):
        j = t // 2
        rows = pl.ds(pl.multiple_of(lax.rem(t, 2) * half_rows, 16), half_rows)
        x = xe[rows, :]
        gate = mm(x, wg[j])
        up = mm(x, wu[j])
        act = (gate / (1.0 + jnp.exp(-gate)) * up).astype(BF16)
        ye[rows, :] += mm(act, wd[j])
        return carry

    lax.fori_loop(0, 8, expert_step, 0)

    def pack(jj):
        gz = lax.rem(cz + dz_of(jj), nz)
        rows = pl.ds(pl.multiple_of(gz * BLK, 16), BLK)
        parts = []
        for i in range(4):
            parts.append(
                jnp.concatenate(
                    [ye[rows, (q * 4 + i) * 128 : (q * 4 + i + 1) * 128] for q in range(4)], axis=1
                ).astype(BF16)
            )
        o = mm(perm2[...], jnp.concatenate(parts, axis=0)).astype(BF16)
        at = pl.multiple_of(gz * nx * BLK, 16)
        for q in range(4):
            send2[q, pl.ds(at, nx * BLK), :] = o[:, q * 128 : (q + 1) * 128]

    pack(0)

    def pack_step(jj, carry):
        pack(jj)
        send_all(d2_copy, jj - 1)
        return carry

    lax.fori_loop(1, nz, pack_step, 0)
    send_all(d2_copy, nz - 1, last=True)

    for jj in range(nz):
        d_wait(recv2.at[pl.ds(0, 4 * nx * BLK)], d2_r.at[jj])

    def collect(b, carry):
        x = jnp.concatenate(
            [recv2[pl.ds(pl.multiple_of((b * 4 + i) * 4 * BLK, 16), 4 * BLK), :] for i in range(4)],
            axis=1,
        )
        o = mm(perm1[...], x).astype(BF16)
        for i in range(4):
            to = pl.multiple_of((b * 4 + i) * BLK, 16)
            for q in range(4):
                zbuf[pl.ds(to, BLK), q * 128 : (q + 1) * 128] = o[
                    q * BLK : (q + 1) * BLK, i * 128 : (i + 1) * 128
                ]
        return carry

    lax.fori_loop(0, nx * nz // 4, collect, 0)
    moe = mm(w_hi[...], zbuf[...]) + mm(w_lo[...], zbuf[...])
    out[...] = (resid[...] + moe).astype(BF16)

    for k in (1, 2, 3):
        ag_copy(k).wait_send()
        rs_copy(k).wait_send()
        st_copy(k).wait_send()
    for a in range(3):
        for i in range(2):
            @pl.when(2 * core + i != my)
            def _():
                w_remote(a, i).wait_send()

    @pl.when(primary)
    def _():
        for a in range(3):
            for j in range(4):
                w_forward(a, j).wait_send()

    sent = pl.ds(0, (n_world - 1) * BLK)
    d_wait(send1.at[sent], d1_s)
    d_wait(recv2.at[sent], d2_s)


def perm_tables():
    index = np.arange(4 * BLK)
    l, b, c = index // BLK, (index % BLK) // CAP, index % CAP
    table = np.zeros((4 * BLK, 4 * BLK), np.float32)
    table[index, b * BLK + l * CAP + c] = 1.0
    return table, table.T.copy()


def body(
    nx, nz,
    hidden_in, norm_in_gain, q_weight, k_weight, v_weight, q_gain, k_gain, o_weight,
    key_pages, value_pages, page_table, cache_len, norm_post_gain, expert_ids, route_weights,
    gate_weight, up_weight, down_weight,
):
    n_chip = nx * nz
    n_world = n_chip * 4
    n_rows = n_world * CAP
    width = hidden_in.shape[1]
    model = norm_in_gain.shape[0]
    ff = gate_weight.shape[2]
    cos_t, sin_t = rope_tables(token_layout(cache_len), 128)
    owner = page_slots(page_table, cache_len).reshape(POOL * PAGE // CHUNK, 1, CHUNK)
    slots = np.arange(n_rows)
    exp_t = (slots[:, None] // CAP == np.arange(TOK)[None, :]).astype(np.float32)
    slot_t = np.broadcast_to((slots % CAP)[:, None], (n_rows, TOK)).astype(np.float32)
    p1, p2 = perm_tables()
    small = [
        hidden_in, norm_in_gain[None, :], q_gain[None, :], k_gain[None, :],
        norm_post_gain.reshape(4, 1, width), cos_t, sin_t, owner,
        expert_ids.T, expert_ids, route_weights,
        jnp.asarray(exp_t, BF16), jnp.asarray(slot_t, BF16), jnp.asarray(exp_t.T, BF16),
        jnp.asarray((slots % CAP)[None, :], F32), jnp.asarray(p1, BF16), jnp.asarray(p2, BF16),
    ]
    cache = POOL * PAGE
    large = [
        q_weight, k_weight, v_weight, o_weight,
        key_pages.reshape(cache, 128), value_pages.reshape(cache, 128),
        gate_weight, up_weight, down_weight,
    ]
    vmem = lambda shape, dtype=BF16: pltpu.VMEM(shape, dtype)
    dma = pltpu.SemaphoreType.DMA
    rows = n_chip * CAP
    return pl.pallas_call(
        functools.partial(layer_kernel, nx, nz),
        out_shape=jax.ShapeDtypeStruct((TOK, width), BF16),
        in_specs=[pl.BlockSpec(memory_space=pltpu.VMEM)] * len(small)
        + [pl.BlockSpec(memory_space=pl.ANY)] * len(large),
        out_specs=pl.BlockSpec(memory_space=pltpu.VMEM),
        scratch_shapes=[
            vmem((4, TOK, width)), vmem((TOK, model)),
            vmem(q_weight.shape), vmem(k_weight.shape), vmem(v_weight.shape), vmem(o_weight.shape),
            vmem((cache, 128)), vmem((cache, 128)),
            vmem((4 * TOK, 128)), vmem((TOK, 128)), vmem((TOK, 128)), vmem((TOK, 512)),
            vmem((4, TOK, width)), vmem((3, TOK, width)),
            vmem((8, TOK), F32), vmem((3, 8, TOK), F32),
            vmem((TOK, width)), vmem((TOK, width), F32),
            vmem((n_rows, TOK)), vmem((TOK, n_rows)), vmem((TOK, n_rows)),
            vmem((n_world * BLK, 128)), vmem((4, n_chip * BLK, 128)),
            vmem((n_rows, width)), vmem((rows, model)),
            vmem((4, model, ff)), vmem((4, model, ff)), vmem((4, ff, model)),
            vmem((rows, model), F32),
            vmem((4, n_chip * BLK, 128)), vmem((n_world * BLK, 128)),
            dma((6,)), dma((3,)), dma((3,)), dma((3,)), dma((3,)), dma((3,)), dma((3,)),
            dma, dma((nz,)), dma, dma((nz,)), dma((3, 2)), dma((3, 4)), dma((3, 4)),
        ],
        compiler_params=pltpu.CompilerParams(
            collective_id=0, has_side_effects=True, vmem_limit_bytes=62 * 1024 * 1024
        ),
    )(*small, *large)


def solution(mesh):
    nx = 4
    nz = mesh.shape["req"] // (2 * nx)
    return jax.shard_map(
        functools.partial(body, nx, nz),
        mesh=mesh,
        in_specs=(
            P("req", "tp"), P(), P(None, "tp"), P(None, "tp"), P(None, "tp"), P(), P(),
            P("tp", None), P("tp", "req", None, None), P("tp", "req", None, None),
            P("req", None), P("req"), P(), P("req", None), P("req", None),
            P("req", None, "tp"), P("req", None, "tp"), P("req", "tp", None),
        ),
        out_specs=P("req", "tp"),
        check_vma=False,
    )
```

```python
import functools
import math

import jax
import jax.numpy as jnp
import numpy as np
from jax import lax
from jax.experimental import pallas as pl
from jax.experimental.pallas import tpu as pltpu
from jax.sharding import PartitionSpec as P

PAGE = 128
MAXPG = 32
PRE = 120
TOK = 128
REQS_DEV = 9
POOL = 48
CAP = 12
NORM_EPS = 1e-06
ROPE_BASE = 1000000.0

MESH = pl.DeviceIdType.MESH
F32 = jnp.float32
BF16 = jnp.bfloat16
BLK = 48
CHUNK = 512


def mm(a, b):
    return jnp.dot(a, b, preferred_element_type=F32)


def mm_t(a, b):
    return lax.dot_general(a, b, (((1,), (1,)), ((), ())), preferred_element_type=F32)


def iota(shape, dim):
    return lax.broadcasted_iota(jnp.int32, shape, dim)


def layer_kernel(
    nx, nz,
    lens, hid, gin, qgain, kgain, gpost, freq, table, ids_t, rw_t,
    exp_t, slot_t, exp_r, slot_r, perm1, perm2,
    qw, kw, vw, ow, kp, vp, wg_in, wu_in, wd_in,
    out,
    owner, cos_t, sin_t, xbuf, nbuf, qw_v, kw_v, vw_v, ow_v, kc, vc, q2, kn, vn, abuf,
    rs_send, rs_recv, st_send, st_recv, nb, resid, s_mat, w_hi, w_lo,
    send1, recv1, zbuf, xe, wg, wu, wd, ye, send2, recv2,
    loc_s, ag_s, ag_r, rs_s, rs_r, st_s, st_r, d1_s, d1_r, d2_s, d2_r, w_s, w_r, f_s,
):
    me_r = lax.axis_index("req")
    my = lax.axis_index("tp")
    core = lax.rem(me_r, 2)
    chip = me_r // 2
    cx = chip // nz
    cz = lax.rem(chip, nz)
    world = chip * 4 + my
    n_world = nx * nz * 4
    n_rows = n_world * CAP
    src_slot = cz * nx + cx

    def peer(k):
        return lax.rem(my + k, 4)

    barrier = pltpu.get_barrier_semaphore()

    def greet(k, carry):
        other = lax.rem(world + k, n_world)
        pl.semaphore_signal(
            barrier, inc=1,
            device_id={"req": (other // 4) * 2 + core, "tp": lax.rem(other, 4)},
            device_id_type=MESH,
        )
        return carry

    lax.fori_loop(1, n_world, greet, 0)
    sibling = {"req": chip * 2 + 1 - core, "tp": my}
    pl.semaphore_signal(barrier, inc=1, device_id=sibling, device_id_type=MESH)

    loads = [
        pltpu.make_async_copy(s, d, loc_s.at[i])
        for i, (s, d) in enumerate(
            [(qw, qw_v), (kw, kw_v), (vw, vw_v), (kp, kc), (vp, vc), (ow, ow_v)]
        )
    ]
    for load in loads:
        load.start()
    xbuf[my] = hid[...]

    lane = iota((TOK, TOK), 1)
    sub = iota((TOK, TOK), 0)
    named_t = jnp.zeros((TOK, TOK), F32)
    dense_t = jnp.zeros((TOK, TOK), F32)
    for k in range(8):
        hit = (ids_t[k : k + 1, :] == sub).astype(F32)
        named_t = named_t + hit
        dense_t = dense_t + hit * rw_t[k : k + 1, :]
    before = (sub < lane).astype(BF16)
    rank_t = jnp.where(named_t > 0, mm(named_t.astype(BF16), before), -1.0)
    s_mat[...] = (mm(exp_t[...], rank_t.astype(BF16)) == slot_t[...].astype(F32)).astype(BF16)
    chosen = mm(rank_t.T.astype(BF16), exp_r[...]) == slot_r[...]
    dense_w = dense_t.T
    dw_hi = dense_w.astype(BF16)
    dw_lo = (dense_w - dw_hi.astype(F32)).astype(BF16)
    w_hi[...] = jnp.where(chosen, mm(dw_hi, exp_r[...]), 0.0).astype(BF16)
    w_lo[...] = jnp.where(chosen, mm(dw_lo, exp_r[...]), 0.0).astype(BF16)

    page = iota((POOL, MAXPG), 0)
    entry = iota((POOL, MAXPG), 1)
    own_sum = jnp.zeros((POOL, MAXPG), jnp.int32)
    start_sum = jnp.zeros((POOL, MAXPG), jnp.int32)
    len_sum = jnp.zeros((POOL, MAXPG), jnp.int32)
    tok_col = iota((TOK, 64), 0)
    tok_req = jnp.where(tok_col < PRE, 0, tok_col - PRE + 1)
    position = jnp.where(tok_col < PRE, tok_col, 0)
    for r in range(REQS_DEV):
        length = lens[r]
        match = (table[r : r + 1, :] == page) & (entry * PAGE < length)
        own_sum = own_sum + jnp.where(match, r + 1, 0)
        start_sum = start_sum + jnp.where(match, entry * PAGE, 0)
        len_sum = len_sum + jnp.where(match, length, 0)
        position = position + jnp.where(tok_req == r, length, 0)

    def lane_sum(v):
        return jnp.sum(v.astype(F32), axis=1, keepdims=True).astype(jnp.int32)

    slot_pos = lane_sum(start_sum) + iota((POOL, PAGE), 1)
    own_col = lane_sum(own_sum)
    owner[...] = jnp.where((own_col > 0) & (slot_pos < lane_sum(len_sum)), own_col - 1, -1)
    angle = position.astype(F32) * freq[...]
    cosine, sine = jnp.cos(angle), jnp.sin(angle)
    cos_t[...] = jnp.concatenate([cosine, cosine], axis=1)
    sin_t[...] = jnp.concatenate([-sine, sine], axis=1)

    pl.semaphore_wait(barrier, n_world)

    def ag_copy(k):
        return pltpu.make_async_remote_copy(
            src_ref=hid, dst_ref=xbuf.at[my], send_sem=ag_s.at[k - 1], recv_sem=ag_r.at[k - 1],
            device_id={"tp": peer(k)}, device_id_type=MESH,
        )

    for k in (1, 3, 2):
        ag_copy(k).start()

    w_pairs = ((wg_in, wg), (wu_in, wu), (wd_in, wd))

    def w_remote(a, i):
        return pltpu.make_async_remote_copy(
            src_ref=w_pairs[a][0].at[i], dst_ref=w_pairs[a][1].at[my],
            send_sem=w_s.at[a, i], recv_sem=w_r.at[a, my],
            device_id={"tp": 2 * core + i}, device_id_type=MESH,
        )

    def w_start(a):
        for i in range(2):
            @pl.when(2 * core + i != my)
            def _():
                w_remote(a, i).start()

            @pl.when(2 * core + i == my)
            def _():
                pltpu.make_async_copy(
                    w_pairs[a][0].at[i], w_pairs[a][1].at[my], w_r.at[a, my]
                ).start()

    def w_forward(a, j):
        return pltpu.make_async_remote_copy(
            src_ref=w_pairs[a][1].at[j], dst_ref=w_pairs[a][1].at[j],
            send_sem=f_s.at[a, j], recv_sem=w_r.at[a, j],
            device_id=sibling, device_id_type=MESH,
        )

    def w_wait(a, j):
        ref = w_pairs[a][1].at[j]
        pltpu.make_async_copy(ref, ref, w_r.at[a, j]).wait()

    primary = core == my // 2

    def w_pass_on(a):
        @pl.when(primary)
        def _():
            for j in range(4):
                w_wait(a, j)
                w_forward(a, j).start()

    w_start(0)

    for k in (1, 3, 2):
        ag_copy(k).wait_recv()
    x_all = jnp.concatenate([xbuf[j].astype(F32) for j in range(4)], axis=1)
    mean_sq = jnp.mean(x_all * x_all, axis=-1, keepdims=True)
    nbuf[...] = (x_all * lax.rsqrt(mean_sq + NORM_EPS) * gin[...]).astype(BF16)
    for load in loads[:3]:
        load.wait()

    def head_norm(v, gain):
        ms = jnp.mean(v * v, axis=-1, keepdims=True)
        v = v * lax.rsqrt(ms + NORM_EPS) * gain
        return (v * cos_t[...] + pltpu.roll(v, 64, 1) * sin_t[...]).astype(BF16)

    q_lin = mm(nbuf[...], qw_v[...])
    for g in range(4):
        q2[g * TOK : (g + 1) * TOK, :] = head_norm(q_lin[:, g * 128 : (g + 1) * 128], qgain[...])
    kn[...] = head_norm(mm(nbuf[...], kw_v[...]), kgain[...])
    vn[...] = mm(nbuf[...], vw_v[...]).astype(BF16)

    inv_root = 1.0 / math.sqrt(128)
    n_q = 4 * TOK
    row_tok = lax.rem(iota((n_q, 1), 0), TOK)
    row_req = jnp.where(row_tok < PRE, 0, row_tok - PRE + 1)
    key_tok = iota((n_q, TOK), 1)
    new_mask = (key_tok == row_tok) | ((row_tok < PRE) & (key_tok <= row_tok))
    sc = jnp.where(new_mask, mm_t(q2[...], kn[...]) * inv_root, -1e30)
    m0 = jnp.max(sc, axis=-1, keepdims=True)
    pr = jnp.exp(sc - m0)
    l0 = jnp.sum(pr, axis=-1, keepdims=True)
    acc0 = mm(pr.astype(BF16), vn[...])
    for load in loads[3:5]:
        load.wait()

    def attend_chunk(j, carry):
        m, l, acc = carry
        at = pl.multiple_of(j * CHUNK, CHUNK)
        s = mm_t(q2[...], kc[pl.ds(at, CHUNK), :]) * inv_root
        own = jnp.concatenate(
            [owner[pl.ds(j * (CHUNK // PAGE) + i, 1), :] for i in range(CHUNK // PAGE)], axis=1
        )
        s = jnp.where(own == row_req, s, -1e30)
        m_new = jnp.maximum(m, jnp.max(s, axis=-1, keepdims=True))
        scale = jnp.exp(m - m_new)
        p = jnp.exp(s - m_new)
        l = l * scale + jnp.sum(p, axis=-1, keepdims=True)
        acc = acc * scale + mm(p.astype(BF16), vc[pl.ds(at, CHUNK), :])
        return m_new, l, acc

    _, l_all, acc_all = lax.fori_loop(0, POOL * PAGE // CHUNK, attend_chunk, (m0, l0, acc0))
    att = (acc_all / l_all).astype(BF16)
    for g in range(4):
        abuf[:, g * 128 : (g + 1) * 128] = att[g * TOK : (g + 1) * TOK, :]
    loads[5].wait()
    for j in range(4):
        rs_send[j] = mm(abuf[...], ow_v[:, j * 512 : (j + 1) * 512]).astype(BF16)

    def rs_copy(k):
        return pltpu.make_async_remote_copy(
            src_ref=rs_send.at[peer(k)], dst_ref=rs_recv.at[k - 1],
            send_sem=rs_s.at[k - 1], recv_sem=rs_r.at[k - 1],
            device_id={"tp": peer(k)}, device_id_type=MESH,
        )

    for k in (1, 3, 2):
        rs_copy(k).start()
    total = hid[...].astype(F32) + rs_send[my].astype(F32)
    for k in (1, 3, 2):
        rs_copy(k).wait_recv()
        total = total + rs_recv[k - 1].astype(F32)
    resid[...] = total
    col = jnp.sum(total * total, axis=-1, keepdims=True)
    diag = sub == lane
    row = jnp.sum(jnp.where(diag, col, 0.0), axis=0, keepdims=True)
    st_send[...] = jnp.broadcast_to(row, (8, TOK))

    def st_copy(k):
        return pltpu.make_async_remote_copy(
            src_ref=st_send, dst_ref=st_recv.at[k - 1],
            send_sem=st_s.at[k - 1], recv_sem=st_r.at[k - 1],
            device_id={"tp": peer(k)}, device_id_type=MESH,
        )

    for k in (1, 3, 2):
        st_copy(k).start()
    w_start(1)
    w_start(2)
    for k in (1, 3, 2):
        st_copy(k).wait_recv()
    row = st_send[0:1, :] + st_recv[0, 0:1, :] + st_recv[1, 0:1, :] + st_recv[2, 0:1, :]
    col = jnp.sum(jnp.where(diag, row, 0.0), axis=-1, keepdims=True)
    nb[...] = (
        resid[...] * lax.rsqrt(col * (1.0 / 2048.0) + NORM_EPS) * gpost[my]
    ).astype(BF16)

    def dz_of(jj):
        return lax.rem(nz // 2 + ((jj + 1) // 2) * (1 - 2 * lax.rem(jj, 2)) + nz, nz)

    def chip_at(jj, dx):
        return lax.rem(cx + dx, nx), lax.rem(cz + dz_of(jj), nz)

    def d1_copy(jj, dx, k, local=False):
        gx, gz = chip_at(jj, dx)
        g = gx * nz + gz
        src = send1.at[pl.ds(pl.multiple_of((g * 4 + peer(k)) * BLK, 16), BLK)]
        dst = recv1.at[my, pl.ds(pl.multiple_of(src_slot * BLK, 16), BLK)]
        if local:
            return pltpu.make_async_copy(src, dst, d1_r.at[jj])
        return pltpu.make_async_remote_copy(
            src_ref=src, dst_ref=dst, send_sem=d1_s, recv_sem=d1_r.at[jj],
            device_id={"req": g * 2 + core, "tp": peer(k)}, device_id_type=MESH,
        )

    def d2_copy(jj, dx, k, local=False):
        gx, gz = chip_at(jj, dx)
        src = send2.at[peer(k), pl.ds(pl.multiple_of((gz * nx + gx) * BLK, 16), BLK)]
        dst = recv2.at[pl.ds(pl.multiple_of(world * BLK, 16), BLK)]
        if local:
            return pltpu.make_async_copy(src, dst, d2_r.at[jj])
        return pltpu.make_async_remote_copy(
            src_ref=src, dst_ref=dst, send_sem=d2_s, recv_sem=d2_r.at[jj],
            device_id={"req": (gx * nz + gz) * 2 + core, "tp": peer(k)}, device_id_type=MESH,
        )

    def send_all(copy_of, jj, last=False):
        for dx in range(nx):
            for k in range(4):
                copy_of(jj, dx, k, local=last and dx == 0 and k == 0).start()

    def build(jj):
        parts = []
        for dx in range(nx):
            gx, gz = chip_at(jj, dx)
            at = pl.multiple_of((gx * nz + gz) * BLK, 16)
            z = mm(s_mat[pl.ds(at, BLK), :], nb[...]).astype(BF16)
            parts.append(jnp.concatenate([z[:, i * 128 : (i + 1) * 128] for i in range(4)], axis=0))
        o = mm(perm2[...], jnp.concatenate(parts, axis=1)).astype(BF16)
        for dx in range(nx):
            gx, gz = chip_at(jj, dx)
            at = pl.multiple_of((gx * nz + gz) * 4 * BLK, 16)
            send1[pl.ds(at, 4 * BLK), :] = o[:, dx * 128 : (dx + 1) * 128]

    build(0)

    def build_step(jj, carry):
        build(jj)
        send_all(d1_copy, jj - 1)
        return carry

    lax.fori_loop(1, nz, build_step, 0)
    send_all(d1_copy, nz - 1, last=True)

    w_pass_on(0)
    w_pass_on(1)
    w_pass_on(2)

    def d_wait(ref, sem):
        pltpu.make_async_copy(ref, ref, sem).wait()

    for jj in range(nz):
        d_wait(recv1.at[0, pl.ds(0, 4 * nx * BLK)], d1_r.at[jj])

    def unpack(gz, carry):
        at = pl.multiple_of(gz * nx * BLK, 16)
        x = jnp.concatenate([recv1[q, pl.ds(at, nx * BLK), :] for q in range(4)], axis=1)
        o = mm(perm1[...], x).astype(BF16)
        to = pl.multiple_of(gz * BLK, 16)
        for q in range(4):
            for i in range(4):
                xe[pl.ds(to, BLK), (q * 4 + i) * 128 : (q * 4 + i + 1) * 128] = o[
                    i * BLK : (i + 1) * BLK, q * 128 : (q + 1) * 128
                ]
        return carry

    lax.fori_loop(0, nz, unpack, 0)

    @pl.when(jnp.logical_not(primary))
    def _():
        for a in range(3):
            for j in range(4):
                w_wait(a, j)

    half_rows = nx * nz * CAP // 2
    ye[...] = jnp.zeros_like(ye)

    def expert_step(t, carry):
        j = t // 2
        rows = pl.ds(pl.multiple_of(lax.rem(t, 2) * half_rows, 16), half_rows)
        x = xe[rows, :]
        gate = mm_t(x, wg[j])
        up = mm_t(x, wu[j])
        act = (gate / (1.0 + jnp.exp(-gate)) * up).astype(BF16)
        ye[rows, :] += mm(act, wd[j])
        return carry

    lax.fori_loop(0, 8, expert_step, 0)

    def pack(jj):
        gz = lax.rem(cz + dz_of(jj), nz)
        rows = pl.ds(pl.multiple_of(gz * BLK, 16), BLK)
        parts = []
        for i in range(4):
            parts.append(
                jnp.concatenate(
                    [ye[rows, (q * 4 + i) * 128 : (q * 4 + i + 1) * 128] for q in range(4)], axis=1
                ).astype(BF16)
            )
        o = mm(perm2[...], jnp.concatenate(parts, axis=0)).astype(BF16)
        at = pl.multiple_of(gz * nx * BLK, 16)
        for q in range(4):
            send2[q, pl.ds(at, nx * BLK), :] = o[:, q * 128 : (q + 1) * 128]

    pack(0)

    def pack_step(jj, carry):
        pack(jj)
        send_all(d2_copy, jj - 1)
        return carry

    lax.fori_loop(1, nz, pack_step, 0)
    send_all(d2_copy, nz - 1, last=True)

    for jj in range(nz):
        d_wait(recv2.at[pl.ds(0, 4 * nx * BLK)], d2_r.at[jj])

    def collect(b, carry):
        x = jnp.concatenate(
            [recv2[pl.ds(pl.multiple_of((b * 4 + i) * 4 * BLK, 16), 4 * BLK), :] for i in range(4)],
            axis=1,
        )
        o = mm(perm1[...], x).astype(BF16)
        for i in range(4):
            to = pl.multiple_of((b * 4 + i) * BLK, 16)
            for q in range(4):
                zbuf[pl.ds(to, BLK), q * 128 : (q + 1) * 128] = o[
                    q * BLK : (q + 1) * BLK, i * 128 : (i + 1) * 128
                ]
        return carry

    lax.fori_loop(0, nx * nz // 4, collect, 0)
    moe = mm(w_hi[...], zbuf[...]) + mm(w_lo[...], zbuf[...])
    out[...] = (resid[...] + moe).astype(BF16)

    for k in (1, 2, 3):
        ag_copy(k).wait_send()
        rs_copy(k).wait_send()
        st_copy(k).wait_send()
    for a in range(3):
        for i in range(2):
            @pl.when(2 * core + i != my)
            def _():
                w_remote(a, i).wait_send()

    @pl.when(primary)
    def _():
        for a in range(3):
            for j in range(4):
                w_forward(a, j).wait_send()

    sent = pl.ds(0, (n_world - 1) * BLK)
    d_wait(send1.at[sent], d1_s)
    d_wait(recv2.at[sent], d2_s)


def perm_tables():
    index = np.arange(4 * BLK)
    l, b, c = index // BLK, (index % BLK) // CAP, index % CAP
    table = np.zeros((4 * BLK, 4 * BLK), np.float32)
    table[index, b * BLK + l * CAP + c] = 1.0
    return table, table.T.copy()


def body(
    nx, nz,
    hidden_in, norm_in_gain, q_weight, k_weight, v_weight, q_gain, k_gain, o_weight,
    key_pages, value_pages, page_table, cache_len, norm_post_gain, expert_ids, route_weights,
    gate_weight, up_weight, down_weight,
):
    n_chip = nx * nz
    n_world = n_chip * 4
    n_rows = n_world * CAP
    width = hidden_in.shape[1]
    model = norm_in_gain.shape[0]
    ff = gate_weight.shape[2]
    half = np.arange(64, dtype=np.float64)
    freq = np.power(ROPE_BASE, -2.0 * half / 128.0)
    slots = np.arange(n_rows)
    exp_t = (slots[:, None] // CAP == np.arange(TOK)[None, :]).astype(np.float32)
    slot_t = np.broadcast_to((slots % CAP)[:, None], (n_rows, TOK)).astype(np.float32)
    p1, p2 = perm_tables()
    small = [
        hidden_in, norm_in_gain[None, :], q_gain[None, :], k_gain[None, :],
        norm_post_gain.reshape(4, 1, width), jnp.asarray(freq[None, :], F32), page_table,
        expert_ids.T, route_weights.T,
        jnp.asarray(exp_t, BF16), jnp.asarray(slot_t, BF16), jnp.asarray(exp_t.T, BF16),
        jnp.asarray((slots % CAP)[None, :], F32), jnp.asarray(p1, BF16), jnp.asarray(p2, BF16),
    ]
    cache = POOL * PAGE
    large = [
        q_weight, k_weight, v_weight, o_weight,
        key_pages.reshape(cache, 128), value_pages.reshape(cache, 128),
        jnp.swapaxes(gate_weight, 1, 2), jnp.swapaxes(up_weight, 1, 2), down_weight,
    ]
    vmem = lambda shape, dtype=BF16: pltpu.VMEM(shape, dtype)
    dma = pltpu.SemaphoreType.DMA
    rows = n_chip * CAP
    return pl.pallas_call(
        functools.partial(layer_kernel, nx, nz),
        out_shape=jax.ShapeDtypeStruct((TOK, width), BF16),
        in_specs=[pl.BlockSpec(memory_space=pltpu.SMEM)]
        + [pl.BlockSpec(memory_space=pltpu.VMEM)] * len(small)
        + [pl.BlockSpec(memory_space=pl.ANY)] * len(large),
        out_specs=pl.BlockSpec(memory_space=pltpu.VMEM),
        scratch_shapes=[
            vmem((POOL, PAGE), jnp.int32), vmem((TOK, 128), F32), vmem((TOK, 128), F32),
            vmem((4, TOK, width)), vmem((TOK, model)),
            vmem(q_weight.shape), vmem(k_weight.shape), vmem(v_weight.shape), vmem(o_weight.shape),
            vmem((cache, 128)), vmem((cache, 128)),
            vmem((4 * TOK, 128)), vmem((TOK, 128)), vmem((TOK, 128)), vmem((TOK, 512)),
            vmem((4, TOK, width)), vmem((3, TOK, width)),
            vmem((8, TOK), F32), vmem((3, 8, TOK), F32),
            vmem((TOK, width)), vmem((TOK, width), F32),
            vmem((n_rows, TOK)), vmem((TOK, n_rows)), vmem((TOK, n_rows)),
            vmem((n_world * BLK, 128)), vmem((4, n_chip * BLK, 128)),
            vmem((n_rows, width)), vmem((rows, model)),
            vmem((4, ff, model)), vmem((4, ff, model)), vmem((4, ff, model)),
            vmem((rows, model), F32),
            vmem((4, n_chip * BLK, 128)), vmem((n_world * BLK, 128)),
            dma((6,)), dma((3,)), dma((3,)), dma((3,)), dma((3,)), dma((3,)), dma((3,)),
            dma, dma((nz,)), dma, dma((nz,)), dma((3, 2)), dma((3, 4)), dma((3, 4)),
        ],
        compiler_params=pltpu.CompilerParams(
            collective_id=0, has_side_effects=True, vmem_limit_bytes=62 * 1024 * 1024
        ),
    )(cache_len, *small, *large)


def solution(mesh):
    nx = 4
    nz = mesh.shape["req"] // (2 * nx)
    return jax.shard_map(
        functools.partial(body, nx, nz),
        mesh=mesh,
        in_specs=(
            P("req", "tp"), P(), P(None, "tp"), P(None, "tp"), P(None, "tp"), P(), P(),
            P("tp", None), P("tp", "req", None, None), P("tp", "req", None, None),
            P("req", None), P("req"), P(), P("req", None), P("req", None),
            P("req", None, "tp"), P("req", None, "tp"), P("req", "tp", None),
        ),
        out_specs=P("req", "tp"),
        check_vma=False,
    )
```

```python
import functools
import math

import jax
import jax.numpy as jnp
import numpy as np
from jax import lax
from jax.experimental import pallas as pl
from jax.experimental.pallas import tpu as pltpu
from jax.sharding import PartitionSpec as P

PAGE = 128
MAXPG = 32
PRE = 120
TOK = 128
REQS_DEV = 9
POOL = 48
CAP = 12
NORM_EPS = 1e-06
ROPE_BASE = 1000000.0

MESH = pl.DeviceIdType.MESH
F32 = jnp.float32
BF16 = jnp.bfloat16
BLK = 48
CHUNK = 512


def mm(a, b):
    return jnp.dot(a, b, preferred_element_type=F32)


def mm_t(a, b):
    return lax.dot_general(a, b, (((1,), (1,)), ((), ())), preferred_element_type=F32)


def iota(shape, dim):
    return lax.broadcasted_iota(jnp.int32, shape, dim)


def layer_kernel(
    nx, nz,
    lens, hid, gin, qgain, kgain, gpost, freq, table, ids_t, rw_t,
    home_t, slot_t, home_r, slot_r, perm1, perm2,
    qw, kw, vw, ow, kp, vp, wg_in, wu_in, wd_in,
    out,
    owner, cos_t, sin_t, xbuf, nbuf, qw_v, kw_v, vw_v, ow_v, kc, vc, q2, kn, vn, abuf,
    rs_send, rs_recv, st_send, st_recv, rbuf, resid, s_mat, w_hi, w_lo,
    send1, recv1, ids_all, rw_all, xe, wg, wu, wd, hbuf, ye, send2, recv2, ring_out, ring_in,
    loc_s, ag_s, ag_r, rs_s, rs_r, st_s, st_r, rb_s, rb_r, d1_s, d1_r, d2_s, d2_r, w_s, w_r, f_s, id_s, id_r, rg_s, rg_r,
):
    me_r = lax.axis_index("req")
    my = lax.axis_index("tp")
    core = lax.rem(me_r, 2)
    chip = me_r // 2
    cx = chip // nz
    cz = lax.rem(chip, nz)
    n_chip = nx * nz
    src_slot = cz * nx + cx
    ff = wd.shape[1]

    def peer(k):
        return lax.rem(my + k, 4)

    barrier = pltpu.get_barrier_semaphore()

    def greet(device):
        pl.semaphore_signal(barrier, inc=1, device_id=device, device_id_type=MESH)

    for k in range(1, n_chip):
        greet({"req": lax.rem(chip + k, n_chip) * 2 + core})
    for dx in range(nx):
        for k in (1, 2, 3):
            greet({"req": (lax.rem(cx + dx, nx) * nz + cz) * 2 + core, "tp": peer(k)})
    sibling = {"req": chip * 2 + 1 - core, "tp": my}
    greet(sibling)
    n_peers = n_chip + 3 * nx

    loads = [
        pltpu.make_async_copy(s, d, loc_s.at[i])
        for i, (s, d) in enumerate(
            [(qw, qw_v), (kw, kw_v), (vw, vw_v), (kp, kc), (vp, vc), (ow, ow_v)]
        )
    ]
    for load in loads:
        load.start()
    xbuf[my] = hid[...]

    lane = iota((TOK, TOK), 1)
    sub = iota((TOK, TOK), 0)

    def routes(group_ids, group_rw):
        named = jnp.zeros((TOK, TOK), F32)
        dense = jnp.zeros((TOK, TOK), F32)
        for k in range(8):
            hit = (group_ids[k : k + 1, :] == sub).astype(F32)
            named = named + hit
            dense = dense + hit * group_rw[k : k + 1, :]
        rank = mm(named.astype(BF16), (sub < lane).astype(BF16))
        return jnp.where(named > 0, rank, -1.0), dense

    homes = (home_t[...] + my == iota(home_t.shape, 1)).astype(BF16)
    rank_t, _ = routes(ids_t[...], rw_t[...])
    s_mat[...] = (mm(homes, rank_t.astype(BF16)) == slot_t[...]).astype(BF16)
    ids_all[cz] = ids_t[...]
    rw_all[cz] = rw_t[...]

    page = iota((POOL, MAXPG), 0)
    entry = iota((POOL, MAXPG), 1)
    own_sum = jnp.zeros((POOL, MAXPG), jnp.int32)
    start_sum = jnp.zeros((POOL, MAXPG), jnp.int32)
    len_sum = jnp.zeros((POOL, MAXPG), jnp.int32)
    tok_col = iota((TOK, 64), 0)
    tok_req = jnp.where(tok_col < PRE, 0, tok_col - PRE + 1)
    position = jnp.where(tok_col < PRE, tok_col, 0)
    for r in range(REQS_DEV):
        length = lens[r]
        match = (table[r : r + 1, :] == page) & (entry * PAGE < length)
        own_sum = own_sum + jnp.where(match, r + 1, 0)
        start_sum = start_sum + jnp.where(match, entry * PAGE, 0)
        len_sum = len_sum + jnp.where(match, length, 0)
        position = position + jnp.where(tok_req == r, length, 0)

    def lane_sum(v):
        return jnp.sum(v.astype(F32), axis=1, keepdims=True).astype(jnp.int32)

    slot_pos = lane_sum(start_sum) + iota((POOL, PAGE), 1)
    own_col = lane_sum(own_sum)
    owner[...] = jnp.where((own_col > 0) & (slot_pos < lane_sum(len_sum)), own_col - 1, -1)
    angle = position.astype(F32) * freq[...]
    cosine, sine = jnp.cos(angle), jnp.sin(angle)
    cos_t[...] = jnp.concatenate([cosine, cosine], axis=1)
    sin_t[...] = jnp.concatenate([-sine, sine], axis=1)

    pl.semaphore_wait(barrier, n_peers)

    def ag_copy(k):
        return pltpu.make_async_remote_copy(
            src_ref=hid, dst_ref=xbuf.at[my], send_sem=ag_s.at[k - 1], recv_sem=ag_r.at[k - 1],
            device_id={"tp": peer(k)}, device_id_type=MESH,
        )

    for k in (1, 3, 2):
        ag_copy(k).start()

    def table_copies(k):
        device = {"req": (cx * nz + lax.rem(cz + k, nz)) * 2 + core}
        return [
            pltpu.make_async_remote_copy(
                src_ref=src, dst_ref=dst.at[cz], send_sem=id_s.at[i], recv_sem=id_r.at[i],
                device_id=device, device_id_type=MESH,
            )
            for i, (src, dst) in enumerate([(ids_t, ids_all), (rw_t, rw_all)])
        ]

    for k in range(1, nz):
        for copy in table_copies(k):
            copy.start()

    w_pairs = ((wg_in, wg), (wu_in, wu), (wd_in, wd))

    piece = ff // 3

    def w_remote(a, i, rows):
        return pltpu.make_async_remote_copy(
            src_ref=w_pairs[a][0].at[i, rows], dst_ref=w_pairs[a][1].at[my, rows],
            send_sem=w_s.at[a, i], recv_sem=w_r.at[a, my],
            device_id={"tp": 2 * core + i}, device_id_type=MESH,
        )

    def w_start(a, t):
        rows = pl.ds(t * piece, piece)
        for i in range(2):
            @pl.when(2 * core + i != my)
            def _():
                w_remote(a, i, rows).start()

            @pl.when(2 * core + i == my)
            def _():
                pltpu.make_async_copy(
                    w_pairs[a][0].at[i, rows], w_pairs[a][1].at[my, rows], w_r.at[a, my]
                ).start()

    def w_forward(a, j):
        return pltpu.make_async_remote_copy(
            src_ref=w_pairs[a][1].at[j], dst_ref=w_pairs[a][1].at[j],
            send_sem=f_s.at[a, j], recv_sem=w_r.at[a, j],
            device_id=sibling, device_id_type=MESH,
        )

    def w_wait(a, j):
        ref = w_pairs[a][1].at[j]
        pltpu.make_async_copy(ref, ref, w_r.at[a, j]).wait()

    primary = core == my // 2

    def w_pass_on(a):
        @pl.when(primary)
        def _():
            for off in (0, 1, 3, 2):
                w_wait(a, peer(off))
                w_forward(a, peer(off)).start()

    w_start(0, 0)
    w_start(0, 1)

    for k in (1, 3, 2):
        ag_copy(k).wait_recv()
    x_all = jnp.concatenate([xbuf[j].astype(F32) for j in range(4)], axis=1)
    mean_sq = jnp.mean(x_all * x_all, axis=-1, keepdims=True)
    nbuf[...] = (x_all * lax.rsqrt(mean_sq + NORM_EPS) * gin[...]).astype(BF16)
    for load in loads[:3]:
        load.wait()

    def head_norm(v, gain):
        ms = jnp.mean(v * v, axis=-1, keepdims=True)
        v = v * lax.rsqrt(ms + NORM_EPS) * gain
        return (v * cos_t[...] + pltpu.roll(v, 64, 1) * sin_t[...]).astype(BF16)

    q_lin = mm(nbuf[...], qw_v[...])
    for g in range(4):
        q2[g * TOK : (g + 1) * TOK, :] = head_norm(q_lin[:, g * 128 : (g + 1) * 128], qgain[...])
    kn[...] = head_norm(mm(nbuf[...], kw_v[...]), kgain[...])
    vn[...] = mm(nbuf[...], vw_v[...]).astype(BF16)

    inv_root = 1.0 / math.sqrt(128)
    n_q = 4 * TOK
    row_tok = lax.rem(iota((n_q, 1), 0), TOK)
    row_req = jnp.where(row_tok < PRE, 0, row_tok - PRE + 1)
    key_tok = iota((n_q, TOK), 1)
    new_mask = (key_tok == row_tok) | ((row_tok < PRE) & (key_tok <= row_tok))
    sc = jnp.where(new_mask, mm_t(q2[...], kn[...]) * inv_root, -1e30)
    m0 = jnp.max(sc, axis=-1, keepdims=True)
    pr = jnp.exp(sc - m0)
    l0 = jnp.sum(pr, axis=-1, keepdims=True)
    acc0 = mm(pr.astype(BF16), vn[...])
    for load in loads[3:5]:
        load.wait()

    def attend_chunk(j, carry):
        m, l, acc = carry
        at = pl.multiple_of(j * CHUNK, CHUNK)
        s = mm_t(q2[...], kc[pl.ds(at, CHUNK), :]) * inv_root
        own = jnp.concatenate(
            [owner[pl.ds(j * (CHUNK // PAGE) + i, 1), :] for i in range(CHUNK // PAGE)], axis=1
        )
        s = jnp.where(own == row_req, s, -1e30)
        m_new = jnp.maximum(m, jnp.max(s, axis=-1, keepdims=True))
        scale = jnp.exp(m - m_new)
        p = jnp.exp(s - m_new)
        l = l * scale + jnp.sum(p, axis=-1, keepdims=True)
        acc = acc * scale + mm(p.astype(BF16), vc[pl.ds(at, CHUNK), :])
        return m_new, l, acc

    _, l_all, acc_all = lax.fori_loop(0, POOL * PAGE // CHUNK, attend_chunk, (m0, l0, acc0))
    att = (acc_all / l_all).astype(BF16)
    for g in range(4):
        abuf[:, g * 128 : (g + 1) * 128] = att[g * TOK : (g + 1) * TOK, :]
    loads[5].wait()
    for j in range(4):
        rs_send[j] = mm(abuf[...], ow_v[:, j * 512 : (j + 1) * 512]).astype(BF16)

    def rs_copy(k):
        return pltpu.make_async_remote_copy(
            src_ref=rs_send.at[peer(k)], dst_ref=rs_recv.at[k - 1],
            send_sem=rs_s.at[k - 1], recv_sem=rs_r.at[k - 1],
            device_id={"tp": peer(k)}, device_id_type=MESH,
        )

    for k in (1, 3, 2):
        rs_copy(k).start()
    total = hid[...].astype(F32) + rs_send[my].astype(F32)
    for k in (1, 3, 2):
        rs_copy(k).wait_recv()
        total = total + rs_recv[k - 1].astype(F32)
    resid[...] = total
    rbuf[my] = total.astype(BF16)
    col = jnp.sum(total * total, axis=-1, keepdims=True)
    diag = sub == lane
    row = jnp.sum(jnp.where(diag, col, 0.0), axis=0, keepdims=True)
    st_send[...] = jnp.broadcast_to(row, (8, TOK))

    def rb_copy(k):
        return pltpu.make_async_remote_copy(
            src_ref=rbuf.at[my], dst_ref=rbuf.at[my],
            send_sem=rb_s.at[k - 1], recv_sem=rb_r.at[k - 1],
            device_id={"tp": peer(k)}, device_id_type=MESH,
        )

    def st_copy(k):
        return pltpu.make_async_remote_copy(
            src_ref=st_send, dst_ref=st_recv.at[k - 1],
            send_sem=st_s.at[k - 1], recv_sem=st_r.at[k - 1],
            device_id={"tp": peer(k)}, device_id_type=MESH,
        )

    for k in (1, 3, 2):
        st_copy(k).start()
        rb_copy(k).start()
    w_start(0, 2)
    for a in (1, 2):
        for t in range(3):
            w_start(a, t)
    for k in (1, 3, 2):
        st_copy(k).wait_recv()
        rb_copy(k).wait_recv()
    row = st_send[0:1, :] + st_recv[0, 0:1, :] + st_recv[1, 0:1, :] + st_recv[2, 0:1, :]
    col = jnp.sum(jnp.where(diag, row, 0.0), axis=-1, keepdims=True)
    row_scale = lax.rsqrt(col * (1.0 / 2048.0) + NORM_EPS)
    for j in range(4):
        nbuf[:, j * 512 : (j + 1) * 512] = (
            rbuf[j].astype(F32) * row_scale * gpost[j]
        ).astype(BF16)

    def dz_of(jj):
        return lax.rem(nz // 2 + ((jj + 1) // 2) * (2 * lax.rem(jj, 2) - 1) + nz, nz)

    def plane(jj):
        return lax.rem(cz + dz_of(jj), nz)

    def chip_at(jj, dx):
        return lax.rem(cx + dx, nx), plane(jj)

    def d1_copy(jj, dx, local=False):
        gx, gz = chip_at(jj, dx)
        src = send1.at[pl.ds(pl.multiple_of((gz * nx + gx) * BLK, 16), BLK)]
        dst = recv1.at[pl.ds(pl.multiple_of(src_slot * BLK, 16), BLK)]
        if local:
            return pltpu.make_async_copy(src, dst, d1_r.at[jj])
        return pltpu.make_async_remote_copy(
            src_ref=src, dst_ref=dst, send_sem=d1_s, recv_sem=d1_r.at[jj],
            device_id={"req": (gx * nz + gz) * 2 + core}, device_id_type=MESH,
        )

    def d2_copy(jj, dx, k, local=False):
        gx, gz = chip_at(jj, dx)
        src = send2.at[peer(k), pl.ds(pl.multiple_of((gz * nx + gx) * BLK, 16), BLK)]
        dst = recv2.at[jj, pl.ds(pl.multiple_of((cx * 4 + my) * BLK, 16), BLK)]
        if local:
            return pltpu.make_async_copy(src, dst, d2_r.at[jj])
        return pltpu.make_async_remote_copy(
            src_ref=src, dst_ref=dst, send_sem=d2_s, recv_sem=d2_r.at[jj],
            device_id={"req": (gx * nz + cz) * 2 + core, "tp": peer(k)}, device_id_type=MESH,
        )

    def send_back(jj):
        for dx in (2, 1, 3, 0):
            for k in (2, 1, 3, 0):
                d2_copy(jj, dx, k, local=dx == 0 and k == 0).start()

    def send_line(jj, last=False):
        for dx in range(nx):
            d1_copy(jj, dx, local=last and dx == 0).start()

    def build(jj):
        gz = plane(jj)
        z = mm(s_mat[pl.ds(pl.multiple_of(gz * BLK, 16), BLK), :], nbuf[...]).astype(BF16)
        parts = jnp.concatenate([z[:, i * 512 : (i + 1) * 512] for i in range(4)], axis=0)
        at = pl.multiple_of(gz * nx * BLK, 16)
        send1[pl.ds(at, nx * BLK), :] = mm(perm2[...], parts).astype(BF16)

    build(0)

    def build_step(jj, carry):
        build(jj)
        send_line(jj - 1)
        return carry

    lax.fori_loop(1, nz, build_step, 0)
    send_line(nz - 1, last=True)

    def d_wait(ref, sem):
        pltpu.make_async_copy(ref, ref, sem).wait()

    d_wait(ids_all.at[pl.ds(0, nz - 1)], id_r.at[0])
    d_wait(rw_all.at[pl.ds(0, nz - 1)], id_r.at[1])
    spread = (home_r[...] + 4 * cz == iota((TOK, home_r.shape[1]), 0)).astype(BF16)

    def weigh(jj, carry):
        gz = plane(jj)
        rank_t, dense_t = routes(ids_all[gz], rw_all[gz])
        chosen = mm(rank_t.T.astype(BF16), spread) == slot_r[...]
        dense_w = dense_t.T
        dw_hi = dense_w.astype(BF16)
        dw_lo = (dense_w - dw_hi.astype(F32)).astype(BF16)
        w_hi[jj] = jnp.where(chosen, mm(dw_hi, spread), 0.0).astype(BF16)
        w_lo[jj] = jnp.where(chosen, mm(dw_lo, spread), 0.0).astype(BF16)
        return carry

    lax.fori_loop(0, nz, weigh, 0)

    w_pass_on(0)
    w_pass_on(1)

    def w_wait_all(a):
        @pl.when(jnp.logical_not(primary))
        def _():
            for j in range(4):
                w_wait(a, j)

    def unpack(jj, carry):
        gz = plane(jj)
        o = mm(perm1[...], recv1[pl.ds(pl.multiple_of(gz * nx * BLK, 16), nx * BLK), :]).astype(BF16)
        to = pl.multiple_of(jj * BLK, 16)
        for i in range(4):
            xe[pl.ds(to, BLK), i * 512 : (i + 1) * 512] = o[i * BLK : (i + 1) * BLK, :]
        return carry

    steps = [(nz // 2 + (j + 1) // 2 * (2 * (j % 2) - 1)) % nz for j in range(nz)]
    from_sem = [steps.index((nz - d) % nz) for d in steps]
    half_rows = n_chip * CAP // 2

    for half in range(2):
        first = half * (nz // 2)
        for jj in range(first, first + nz // 2):
            d_wait(recv1.at[pl.ds(0, nx * BLK)], d1_r.at[from_sem[jj]])
        lax.fori_loop(first, first + nz // 2, unpack, 0)
        if half == 0:
            w_wait_all(0)
            w_wait_all(1)
        rows = pl.ds(half * half_rows, half_rows)

        def act_step(j, carry):
            x = xe[rows, :]
            gate = mm_t(x, wg[j])
            up = mm_t(x, wu[j])
            hbuf[j, rows, :] = (gate / (1.0 + jnp.exp(-gate)) * up).astype(BF16)
            return carry

        lax.fori_loop(0, 4, act_step, 0)
        if half == 0:
            w_pass_on(2)
    w_wait_all(2)

    def pack(jj):
        gz = plane(jj)
        rows = pl.ds(pl.multiple_of(jj * BLK, 16), BLK)
        parts = []
        for i in range(4):
            parts.append(
                jnp.concatenate(
                    [ye[rows, (q * 4 + i) * 128 : (q * 4 + i + 1) * 128] for q in range(4)], axis=1
                ).astype(BF16)
            )
        o = mm(perm2[...], jnp.concatenate(parts, axis=0)).astype(BF16)
        at = pl.multiple_of(gz * nx * BLK, 16)
        for q in range(4):
            send2[q, pl.ds(at, nx * BLK), :] = o[:, q * 128 : (q + 1) * 128]

    for half in range(2):
        rows = pl.ds(half * half_rows, half_rows)
        ye[rows, :] = mm(hbuf[0, rows, :], wd[0])

        def down_step(j, carry):
            ye[rows, :] += mm(hbuf[j, rows, :], wd[j])
            return carry

        lax.fori_loop(1, 4, down_step, 0)
        first = half * (nz // 2)
        pack(first)

        def pack_step(jj, carry):
            pack(jj)
            send_back(jj - 1)
            return carry

        lax.fori_loop(first + 1, first + nz // 2, pack_step, 0)
        send_back(first + nz // 2 - 1)

    def ring_copy(jj):
        step = 1 if jj % 2 == 0 else nz - 1
        return pltpu.make_async_remote_copy(
            src_ref=ring_out.at[jj], dst_ref=ring_in.at[jj],
            send_sem=rg_s.at[jj], recv_sem=rg_r.at[jj],
            device_id={"req": (cx * nz + lax.rem(cz + step, nz)) * 2 + core}, device_id_type=MESH,
        )

    def partial_sum(jj):
        d_wait(recv2.at[jj], d2_r.at[jj])
        x = jnp.concatenate(
            [recv2[jj, i * 4 * BLK : (i + 1) * 4 * BLK, :] for i in range(nx)], axis=1
        )
        o = mm(perm1[...], x).astype(BF16)
        rows = [
            jnp.concatenate(
                [o[q * BLK : (q + 1) * BLK, i * 128 : (i + 1) * 128] for q in range(4)], axis=1
            )
            for i in range(nx)
        ]
        back = jnp.concatenate(rows, axis=0)
        return mm(w_hi[jj], back) + mm(w_lo[jj], back)

    for jj in range(nz - 1):
        part = partial_sum(jj)
        if jj >= 2:
            ring_copy(jj - 2).wait_recv()
            part = part + ring_in[jj - 2].astype(F32)
        ring_out[jj] = part.astype(BF16)
        ring_copy(jj).start()
    moe = partial_sum(nz - 1)
    for jj in (nz - 3, nz - 2):
        ring_copy(jj).wait_recv()
        moe = moe + ring_in[jj].astype(F32)
    out[...] = (resid[...] + moe).astype(BF16)

    for k in (1, 2, 3):
        ag_copy(k).wait_send()
        rs_copy(k).wait_send()
        st_copy(k).wait_send()
        rb_copy(k).wait_send()
    for a in range(3):
        for i in range(2):
            @pl.when(2 * core + i != my)
            def _():
                w_remote(a, i, pl.ds(0, ff)).wait_send()

    @pl.when(primary)
    def _():
        for a in range(3):
            for j in range(4):
                w_forward(a, j).wait_send()

    d_wait(send1.at[pl.ds(0, (nx * nz - 1) * BLK)], d1_s)
    for jj in range(nz):
        d_wait(recv2.at[0, pl.ds(0, (nx * 4 - 1) * BLK)], d2_s)
    for jj in range(nz - 1):
        ring_copy(jj).wait_send()
    d_wait(ids_all.at[pl.ds(0, nz - 1)], id_s.at[0])
    d_wait(rw_all.at[pl.ds(0, nz - 1)], id_s.at[1])


def perm_tables():
    index = np.arange(4 * BLK)
    l, b, c = index // BLK, (index % BLK) // CAP, index % CAP
    table = np.zeros((4 * BLK, 4 * BLK), np.float32)
    table[index, b * BLK + l * CAP + c] = 1.0
    return table, table.T.copy()


def body(
    nx, nz,
    hidden_in, norm_in_gain, q_weight, k_weight, v_weight, q_gain, k_gain, o_weight,
    key_pages, value_pages, page_table, cache_len, norm_post_gain, expert_ids, route_weights,
    gate_weight, up_weight, down_weight,
):
    n_chip = nx * nz
    width = hidden_in.shape[1]
    model = norm_in_gain.shape[0]
    ff = gate_weight.shape[2]
    half = np.arange(64, dtype=np.float64)
    freq = np.power(ROPE_BASE, -2.0 * half / 128.0)
    slots = np.arange(nx * 4 * CAP)
    home_r = slots // (4 * CAP) * nz * 4 + slots // CAP % 4
    line = np.arange(n_chip * CAP) // CAP
    home = ((line % nx) * nz + line // nx) * 4
    home_t = np.broadcast_to(home[:, None], (n_chip * CAP, TOK))
    slot_t = np.broadcast_to((np.arange(n_chip * CAP) % CAP)[:, None], (n_chip * CAP, TOK))
    p1, p2 = perm_tables()
    small = [
        hidden_in, norm_in_gain[None, :], q_gain[None, :], k_gain[None, :],
        norm_post_gain.reshape(4, 1, width), jnp.asarray(freq[None, :], F32), page_table,
        expert_ids.T, route_weights.T,
        jnp.asarray(home_t, jnp.int32), jnp.asarray(slot_t, F32),
        jnp.asarray(home_r[None, :], jnp.int32), jnp.asarray((slots % CAP)[None, :], F32), jnp.asarray(p1, BF16), jnp.asarray(p2, BF16),
    ]
    cache = POOL * PAGE
    large = [
        q_weight, k_weight, v_weight, o_weight,
        key_pages.reshape(cache, 128), value_pages.reshape(cache, 128),
        jnp.swapaxes(gate_weight, 1, 2), jnp.swapaxes(up_weight, 1, 2), down_weight,
    ]
    vmem = lambda shape, dtype=BF16: pltpu.VMEM(shape, dtype)
    dma = pltpu.SemaphoreType.DMA
    rows = n_chip * CAP
    return pl.pallas_call(
        functools.partial(layer_kernel, nx, nz),
        out_shape=jax.ShapeDtypeStruct((TOK, width), BF16),
        in_specs=[pl.BlockSpec(memory_space=pltpu.SMEM)]
        + [pl.BlockSpec(memory_space=pltpu.VMEM)] * len(small)
        + [pl.BlockSpec(memory_space=pl.ANY)] * len(large),
        out_specs=pl.BlockSpec(memory_space=pltpu.VMEM),
        scratch_shapes=[
            vmem((POOL, PAGE), jnp.int32), vmem((TOK, 128), F32), vmem((TOK, 128), F32),
            vmem((4, TOK, width)), vmem((TOK, model)),
            vmem(q_weight.shape), vmem(k_weight.shape), vmem(v_weight.shape), vmem(o_weight.shape),
            vmem((cache, 128)), vmem((cache, 128)),
            vmem((4 * TOK, 128)), vmem((TOK, 128)), vmem((TOK, 128)), vmem((TOK, 512)),
            vmem((4, TOK, width)), vmem((3, TOK, width)),
            vmem((8, TOK), F32), vmem((3, 8, TOK), F32),
            vmem((4, TOK, width)), vmem((TOK, width), F32),
            vmem((rows, TOK)), vmem((nz, TOK, nx * 4 * CAP)), vmem((nz, TOK, nx * 4 * CAP)),
            vmem((n_chip * BLK, width)), vmem((n_chip * BLK, width)),
            vmem((nz, 8, TOK), jnp.int32), vmem((nz, 8, TOK), F32), vmem((rows, model)),
            vmem((4, ff, model)), vmem((4, ff, model)), vmem((4, ff, model)),
            vmem((4, rows, ff)), vmem((rows, model), F32),
            vmem((4, n_chip * BLK, 128)), vmem((nz, nx * 4 * BLK, 128)),
            vmem((nz - 1, TOK, width)), vmem((nz - 1, TOK, width)),
            dma((6,)), dma((3,)), dma((3,)), dma((3,)), dma((3,)), dma((3,)), dma((3,)),
            dma((3,)), dma((3,)), dma, dma((nz,)), dma, dma((nz,)), dma((3, 2)), dma((3, 4)), dma((3, 4)),
            dma((2,)), dma((2,)), dma((nz - 1,)), dma((nz - 1,)),
        ],
        compiler_params=pltpu.CompilerParams(
            collective_id=0, has_side_effects=True, vmem_limit_bytes=62 * 1024 * 1024
        ),
    )(cache_len, *small, *large)


def solution(mesh):
    nx = 4
    nz = mesh.shape["req"] // (2 * nx)
    return jax.shard_map(
        functools.partial(body, nx, nz),
        mesh=mesh,
        in_specs=(
            P("req", "tp"), P(), P(None, "tp"), P(None, "tp"), P(None, "tp"), P(), P(),
            P("tp", None), P("tp", "req", None, None), P("tp", "req", None, None),
            P("req", None), P("req"), P(), P("req", None), P("req", None),
            P("req", None, "tp"), P("req", None, "tp"), P("req", "tp", None),
        ),
        out_specs=P("req", "tp"),
        check_vma=False,
    )
```

```python
import functools
import math

import jax
import jax.numpy as jnp
import numpy as np
from jax import lax
from jax.experimental import pallas as pl
from jax.experimental.pallas import tpu as pltpu
from jax.sharding import PartitionSpec as P

PAGE = 128
MAXPG = 32
PRE = 120
TOK = 128
REQS_DEV = 9
POOL = 48
CAP = 12
NORM_EPS = 1e-06
ROPE_BASE = 1000000.0

MESH = pl.DeviceIdType.MESH
F32 = jnp.float32
BF16 = jnp.bfloat16
BLK = 48
CHUNK = 512


def mm(a, b):
    return jnp.dot(a, b, preferred_element_type=F32)


def mm_t(a, b):
    return lax.dot_general(a, b, (((1,), (1,)), ((), ())), preferred_element_type=F32)


def iota(shape, dim):
    return lax.broadcasted_iota(jnp.int32, shape, dim)


def layer_kernel(
    nx, nz,
    lens, hid, gin, qgain, kgain, gpost, freq, table, ids_t, rw_t,
    home_t, slot_t, home_r, slot_r, perm1, perm2,
    qw, kw, vw, ow, kp, vp, wg_in, wu_in, wd_in,
    out,
    owner, cos_t, sin_t, xbuf, nbuf, qw_v, kw_v, vw_v, ow_v, kc, vc, q2, kn, vn, abuf,
    rs_send, rs_recv, st_send, st_recv, rbuf, resid, s_mat, w_hi, w_lo,
    send1, recv1, ids_all, rw_all, xe, wg, wu, wd, hbuf, ye, send2, recv2, ring_out, ring_in,
    loc_s, ag_s, ag_r, rs_s, rs_r, st_s, st_r, rb_s, rb_r, d1_s, d1_r, d2_s, d2_r, w_s, w_r, f_s, id_s, id_r, rg_s, rg_r,
):
    me_r = lax.axis_index("req")
    my = lax.axis_index("tp")
    core = lax.rem(me_r, 2)
    chip = me_r // 2
    cx = chip // nz
    cz = lax.rem(chip, nz)
    n_chip = nx * nz
    src_slot = cz * nx + cx
    ff = wd.shape[1]

    def peer(k):
        return lax.rem(my + k, 4)

    barrier = pltpu.get_barrier_semaphore()

    def greet(device):
        pl.semaphore_signal(barrier, inc=1, device_id=device, device_id_type=MESH)

    for k in range(1, n_chip):
        greet({"req": lax.rem(chip + k, n_chip) * 2 + core})
    for dx in range(nx):
        for k in (1, 2, 3):
            greet({"req": (lax.rem(cx + dx, nx) * nz + cz) * 2 + core, "tp": peer(k)})
    sibling = {"req": chip * 2 + 1 - core, "tp": my}
    greet(sibling)
    n_peers = n_chip + 3 * nx

    loads = [
        pltpu.make_async_copy(s, d, loc_s.at[i])
        for i, (s, d) in enumerate(
            [(qw, qw_v), (kw, kw_v), (vw, vw_v), (kp, kc), (vp, vc), (ow, ow_v)]
        )
    ]
    for load in loads:
        load.start()
    xbuf[my] = hid[...]

    lane = iota((TOK, TOK), 1)
    sub = iota((TOK, TOK), 0)

    def routes(group_ids, group_rw):
        named = jnp.zeros((TOK, TOK), F32)
        dense = jnp.zeros((TOK, TOK), F32)
        for k in range(8):
            hit = (group_ids[k : k + 1, :] == sub).astype(F32)
            named = named + hit
            dense = dense + hit * group_rw[k : k + 1, :]
        rank = mm(named.astype(BF16), (sub < lane).astype(BF16))
        return jnp.where(named > 0, rank, -1.0), dense

    homes = (home_t[...] + my == iota(home_t.shape, 1)).astype(BF16)
    rank_t, _ = routes(ids_t[...], rw_t[...])
    s_mat[...] = (mm(homes, rank_t.astype(BF16)) == slot_t[...]).astype(BF16)
    ids_all[cz] = ids_t[...]
    rw_all[cz] = rw_t[...]

    page = iota((POOL, MAXPG), 0)
    entry = iota((POOL, MAXPG), 1)
    own_sum = jnp.zeros((POOL, MAXPG), jnp.int32)
    start_sum = jnp.zeros((POOL, MAXPG), jnp.int32)
    len_sum = jnp.zeros((POOL, MAXPG), jnp.int32)
    tok_col = iota((TOK, 64), 0)
    tok_req = jnp.where(tok_col < PRE, 0, tok_col - PRE + 1)
    position = jnp.where(tok_col < PRE, tok_col, 0)
    for r in range(REQS_DEV):
        length = lens[r]
        match = (table[r : r + 1, :] == page) & (entry * PAGE < length)
        own_sum = own_sum + jnp.where(match, r + 1, 0)
        start_sum = start_sum + jnp.where(match, entry * PAGE, 0)
        len_sum = len_sum + jnp.where(match, length, 0)
        position = position + jnp.where(tok_req == r, length, 0)

    def lane_sum(v):
        return jnp.sum(v.astype(F32), axis=1, keepdims=True).astype(jnp.int32)

    slot_pos = lane_sum(start_sum) + iota((POOL, PAGE), 1)
    own_col = lane_sum(own_sum)
    owner[...] = jnp.where((own_col > 0) & (slot_pos < lane_sum(len_sum)), own_col - 1, -1)
    angle = position.astype(F32) * freq[...]
    cosine, sine = jnp.cos(angle), jnp.sin(angle)
    cos_t[...] = jnp.concatenate([cosine, cosine], axis=1)
    sin_t[...] = jnp.concatenate([-sine, sine], axis=1)

    pl.semaphore_wait(barrier, n_peers)

    def ag_copy(k):
        return pltpu.make_async_remote_copy(
            src_ref=hid, dst_ref=xbuf.at[my], send_sem=ag_s.at[k - 1], recv_sem=ag_r.at[k - 1],
            device_id={"tp": peer(k)}, device_id_type=MESH,
        )

    for k in (1, 3, 2):
        ag_copy(k).start()

    def table_copies(k):
        device = {"req": (cx * nz + lax.rem(cz + k, nz)) * 2 + core}
        return [
            pltpu.make_async_remote_copy(
                src_ref=src, dst_ref=dst.at[cz], send_sem=id_s.at[i], recv_sem=id_r.at[i],
                device_id=device, device_id_type=MESH,
            )
            for i, (src, dst) in enumerate([(ids_t, ids_all), (rw_t, rw_all)])
        ]

    for k in range(1, nz):
        for copy in table_copies(k):
            copy.start()

    w_pairs = ((wg_in, wg), (wu_in, wu), (wd_in, wd))

    piece = ff // 3

    def w_remote(a, i, rows):
        return pltpu.make_async_remote_copy(
            src_ref=w_pairs[a][0].at[i, rows], dst_ref=w_pairs[a][1].at[my, rows],
            send_sem=w_s.at[a, i], recv_sem=w_r.at[a, my],
            device_id={"tp": 2 * core + i}, device_id_type=MESH,
        )

    def w_start(a, t):
        rows = pl.ds(t * piece, piece)
        for i in range(2):
            @pl.when(2 * core + i != my)
            def _():
                w_remote(a, i, rows).start()

            @pl.when(2 * core + i == my)
            def _():
                pltpu.make_async_copy(
                    w_pairs[a][0].at[i, rows], w_pairs[a][1].at[my, rows], w_r.at[a, my]
                ).start()

    def w_forward(a, j):
        return pltpu.make_async_remote_copy(
            src_ref=w_pairs[a][1].at[j], dst_ref=w_pairs[a][1].at[j],
            send_sem=f_s.at[a, j], recv_sem=w_r.at[a, j],
            device_id=sibling, device_id_type=MESH,
        )

    def w_wait(a, j):
        ref = w_pairs[a][1].at[j]
        pltpu.make_async_copy(ref, ref, w_r.at[a, j]).wait()

    primary = core == my // 2

    def w_pass_on(a, offs=(0, 1, 3, 2)):
        @pl.when(primary)
        def _():
            for off in offs:
                w_wait(a, peer(off))
                w_forward(a, peer(off)).start()

    w_start(0, 0)
    w_start(0, 1)

    for k in (1, 3, 2):
        ag_copy(k).wait_recv()
    x_all = jnp.concatenate([xbuf[j].astype(F32) for j in range(4)], axis=1)
    mean_sq = jnp.mean(x_all * x_all, axis=-1, keepdims=True)
    nbuf[...] = (x_all * lax.rsqrt(mean_sq + NORM_EPS) * gin[...]).astype(BF16)
    for load in loads[:3]:
        load.wait()

    def head_norm(v, gain):
        ms = jnp.mean(v * v, axis=-1, keepdims=True)
        v = v * lax.rsqrt(ms + NORM_EPS) * gain
        return (v * cos_t[...] + pltpu.roll(v, 64, 1) * sin_t[...]).astype(BF16)

    score_scale = math.log2(math.e) / math.sqrt(128)
    q_lin = mm(nbuf[...], qw_v[...])
    for g in range(4):
        q2[g * TOK : (g + 1) * TOK, :] = head_norm(
            q_lin[:, g * 128 : (g + 1) * 128], qgain[...] * score_scale
        )
    kn[...] = head_norm(mm(nbuf[...], kw_v[...]), kgain[...])
    vn[...] = mm(nbuf[...], vw_v[...]).astype(BF16)

    n_q = 4 * TOK
    row_tok = lax.rem(iota((n_q, 1), 0), TOK)
    row_req = jnp.where(row_tok < PRE, 0, row_tok - PRE + 1)
    key_tok = iota((n_q, TOK), 1)
    new_mask = (key_tok == row_tok) | ((row_tok < PRE) & (key_tok <= row_tok))
    sc = jnp.where(new_mask, mm_t(q2[...], kn[...]), -1e30)
    m0 = jnp.max(sc, axis=-1, keepdims=True)
    pr = jnp.exp2(sc - m0)
    l0 = jnp.sum(pr, axis=-1, keepdims=True)
    acc0 = mm(pr.astype(BF16), vn[...])
    for load in loads[3:5]:
        load.wait()

    def attend_chunk(j, carry):
        m, l, acc = carry
        at = pl.multiple_of(j * CHUNK, CHUNK)
        s = mm_t(q2[...], kc[pl.ds(at, CHUNK), :])
        own = jnp.concatenate(
            [owner[pl.ds(j * (CHUNK // PAGE) + i, 1), :] for i in range(CHUNK // PAGE)], axis=1
        )
        s = jnp.where(own == row_req, s, -1e30)
        m_new = jnp.maximum(m, jnp.max(s, axis=-1, keepdims=True))
        scale = jnp.exp2(m - m_new)
        p = jnp.exp2(s - m_new)
        l = l * scale + jnp.sum(p, axis=-1, keepdims=True)
        acc = acc * scale + mm(p.astype(BF16), vc[pl.ds(at, CHUNK), :])
        return m_new, l, acc

    _, l_all, acc_all = lax.fori_loop(
        0, POOL * PAGE // CHUNK, attend_chunk, (m0, l0, acc0), unroll=4
    )
    att = (acc_all / l_all).astype(BF16)
    for g in range(4):
        abuf[:, g * 128 : (g + 1) * 128] = att[g * TOK : (g + 1) * TOK, :]
    loads[5].wait()
    for j in range(4):
        rs_send[j] = mm(abuf[...], ow_v[:, j * 512 : (j + 1) * 512]).astype(BF16)

    def rs_copy(k):
        return pltpu.make_async_remote_copy(
            src_ref=rs_send.at[peer(k)], dst_ref=rs_recv.at[k - 1],
            send_sem=rs_s.at[k - 1], recv_sem=rs_r.at[k - 1],
            device_id={"tp": peer(k)}, device_id_type=MESH,
        )

    for k in (1, 3, 2):
        rs_copy(k).start()
    total = hid[...].astype(F32) + rs_send[my].astype(F32)
    for k in (1, 3, 2):
        rs_copy(k).wait_recv()
        total = total + rs_recv[k - 1].astype(F32)
    resid[...] = total
    rbuf[my] = total.astype(BF16)
    col = jnp.sum(total * total, axis=-1, keepdims=True)
    diag = sub == lane
    row = jnp.sum(jnp.where(diag, col, 0.0), axis=0, keepdims=True)
    st_send[...] = jnp.broadcast_to(row, (8, TOK))

    def rb_copy(k):
        return pltpu.make_async_remote_copy(
            src_ref=rbuf.at[my], dst_ref=rbuf.at[my],
            send_sem=rb_s.at[k - 1], recv_sem=rb_r.at[k - 1],
            device_id={"tp": peer(k)}, device_id_type=MESH,
        )

    def st_copy(k):
        return pltpu.make_async_remote_copy(
            src_ref=st_send, dst_ref=st_recv.at[k - 1],
            send_sem=st_s.at[k - 1], recv_sem=st_r.at[k - 1],
            device_id={"tp": peer(k)}, device_id_type=MESH,
        )

    for k in (1, 3, 2):
        st_copy(k).start()
        rb_copy(k).start()
    w_start(0, 2)
    for a in (1, 2):
        for t in range(3):
            w_start(a, t)
    for k in (1, 3, 2):
        st_copy(k).wait_recv()
        rb_copy(k).wait_recv()
    row = st_send[0:1, :] + st_recv[0, 0:1, :] + st_recv[1, 0:1, :] + st_recv[2, 0:1, :]
    col = jnp.sum(jnp.where(diag, row, 0.0), axis=-1, keepdims=True)
    row_scale = lax.rsqrt(col * (1.0 / 2048.0) + NORM_EPS)
    for j in range(4):
        nbuf[:, j * 512 : (j + 1) * 512] = (
            rbuf[j].astype(F32) * row_scale * gpost[j]
        ).astype(BF16)

    def dz_of(jj):
        return lax.rem(nz // 2 + ((jj + 1) // 2) * (2 * lax.rem(jj, 2) - 1) + nz, nz)

    def plane(jj):
        return lax.rem(cz + dz_of(jj), nz)

    def chip_at(jj, dx):
        return lax.rem(cx + dx, nx), plane(jj)

    def d1_copy(jj, dx, local=False):
        gx, gz = chip_at(jj, dx)
        src = send1.at[pl.ds(pl.multiple_of((gz * nx + gx) * BLK, 16), BLK)]
        dst = recv1.at[pl.ds(pl.multiple_of(src_slot * BLK, 16), BLK)]
        if local:
            return pltpu.make_async_copy(src, dst, d1_r.at[jj])
        return pltpu.make_async_remote_copy(
            src_ref=src, dst_ref=dst, send_sem=d1_s, recv_sem=d1_r.at[jj],
            device_id={"req": (gx * nz + gz) * 2 + core}, device_id_type=MESH,
        )

    def d2_copy(jj, dx, k, local=False):
        gx, gz = chip_at(jj, dx)
        src = send2.at[peer(k), pl.ds(pl.multiple_of((gz * nx + gx) * BLK, 16), BLK)]
        dst = recv2.at[jj, pl.ds(pl.multiple_of((cx * 4 + my) * BLK, 16), BLK)]
        if local:
            return pltpu.make_async_copy(src, dst, d2_r.at[jj])
        return pltpu.make_async_remote_copy(
            src_ref=src, dst_ref=dst, send_sem=d2_s, recv_sem=d2_r.at[jj],
            device_id={"req": (gx * nz + cz) * 2 + core, "tp": peer(k)}, device_id_type=MESH,
        )

    def send_back(jj):
        for dx in (2, 1, 3, 0):
            for k in (2, 1, 3, 0):
                d2_copy(jj, dx, k, local=dx == 0 and k == 0).start()

    def send_line(jj, last=False):
        for dx in range(nx):
            d1_copy(jj, dx, local=last and dx == 0).start()

    def build(jj):
        gz = plane(jj)
        z = mm(s_mat[pl.ds(pl.multiple_of(gz * BLK, 16), BLK), :], nbuf[...]).astype(BF16)
        parts = jnp.concatenate([z[:, i * 512 : (i + 1) * 512] for i in range(4)], axis=0)
        at = pl.multiple_of(gz * nx * BLK, 16)
        send1[pl.ds(at, nx * BLK), :] = mm(perm2[...], parts).astype(BF16)

    build(0)

    def build_step(jj, carry):
        build(jj)
        send_line(jj - 1)
        return carry

    lax.fori_loop(1, nz, build_step, 0)
    send_line(nz - 1, last=True)

    def d_wait(ref, sem):
        pltpu.make_async_copy(ref, ref, sem).wait()

    d_wait(ids_all.at[pl.ds(0, nz - 1)], id_r.at[0])
    d_wait(rw_all.at[pl.ds(0, nz - 1)], id_r.at[1])
    spread = (home_r[...] + 4 * cz == iota((TOK, home_r.shape[1]), 0)).astype(BF16)

    def weigh(jj, carry):
        gz = plane(jj)
        rank_t, dense_t = routes(ids_all[gz], rw_all[gz])
        chosen = mm(rank_t.T.astype(BF16), spread) == slot_r[...]
        dense_w = dense_t.T
        dw_hi = dense_w.astype(BF16)
        dw_lo = (dense_w - dw_hi.astype(F32)).astype(BF16)
        w_hi[jj] = jnp.where(chosen, mm(dw_hi, spread), 0.0).astype(BF16)
        w_lo[jj] = jnp.where(chosen, mm(dw_lo, spread), 0.0).astype(BF16)
        return carry

    lax.fori_loop(0, nz, weigh, 0)

    w_pass_on(0)
    w_pass_on(1)
    w_pass_on(2, (0,))

    def w_wait_all(a):
        @pl.when(jnp.logical_not(primary))
        def _():
            for j in range(4):
                w_wait(a, j)

    def unpack(jj, carry):
        gz = plane(jj)
        o = mm(perm1[...], recv1[pl.ds(pl.multiple_of(gz * nx * BLK, 16), nx * BLK), :]).astype(BF16)
        to = pl.multiple_of(jj * BLK, 16)
        for i in range(4):
            xe[pl.ds(to, BLK), i * 512 : (i + 1) * 512] = o[i * BLK : (i + 1) * BLK, :]
        return carry

    steps = [(nz // 2 + (j + 1) // 2 * (2 * (j % 2) - 1)) % nz for j in range(nz)]
    from_sem = [steps.index((nz - d) % nz) for d in steps]
    half_rows = n_chip * CAP // 2

    for half in range(2):
        first = half * (nz // 2)
        for jj in range(first, first + nz // 2):
            d_wait(recv1.at[pl.ds(0, nx * BLK)], d1_r.at[from_sem[jj]])
        if half == 1:
            w_pass_on(2, (1, 3, 2))
        lax.fori_loop(first, first + nz // 2, unpack, 0)
        if half == 0:
            w_wait_all(0)
            w_wait_all(1)
        rows = pl.ds(half * half_rows, half_rows)

        def act_step(j, carry):
            x = xe[rows, :]
            gate = mm_t(x, wg[j])
            up = mm_t(x, wu[j])
            hbuf[j, rows, :] = (gate / (1.0 + jnp.exp(-gate)) * up).astype(BF16)
            return carry

        lax.fori_loop(0, 4, act_step, 0)
    w_wait_all(2)

    def pack(jj):
        gz = plane(jj)
        rows = pl.ds(pl.multiple_of(jj * BLK, 16), BLK)
        parts = []
        for i in range(4):
            parts.append(
                jnp.concatenate(
                    [ye[rows, (q * 4 + i) * 128 : (q * 4 + i + 1) * 128] for q in range(4)], axis=1
                ).astype(BF16)
            )
        o = mm(perm2[...], jnp.concatenate(parts, axis=0)).astype(BF16)
        at = pl.multiple_of(gz * nx * BLK, 16)
        for q in range(4):
            send2[q, pl.ds(at, nx * BLK), :] = o[:, q * 128 : (q + 1) * 128]

    for half in range(2):
        rows = pl.ds(half * half_rows, half_rows)
        ye[rows, :] = mm(hbuf[0, rows, :], wd[0])

        def down_step(j, carry):
            ye[rows, :] += mm(hbuf[j, rows, :], wd[j])
            return carry

        lax.fori_loop(1, 4, down_step, 0)
        first = half * (nz // 2)
        pack(first)

        def pack_step(jj, carry):
            pack(jj)
            send_back(jj - 1)
            return carry

        lax.fori_loop(first + 1, first + nz // 2, pack_step, 0)
        send_back(first + nz // 2 - 1)

    def ring_copy(jj):
        step = 1 if jj % 2 == 0 else nz - 1
        return pltpu.make_async_remote_copy(
            src_ref=ring_out.at[jj], dst_ref=ring_in.at[jj],
            send_sem=rg_s.at[jj], recv_sem=rg_r.at[jj],
            device_id={"req": (cx * nz + lax.rem(cz + step, nz)) * 2 + core}, device_id_type=MESH,
        )

    def partial_sum(jj):
        d_wait(recv2.at[jj], d2_r.at[jj])
        x = jnp.concatenate(
            [recv2[jj, i * 4 * BLK : (i + 1) * 4 * BLK, :] for i in range(nx)], axis=1
        )
        o = mm(perm1[...], x).astype(BF16)
        rows = [
            jnp.concatenate(
                [o[q * BLK : (q + 1) * BLK, i * 128 : (i + 1) * 128] for q in range(4)], axis=1
            )
            for i in range(nx)
        ]
        back = jnp.concatenate(rows, axis=0)
        return mm(w_hi[jj], back) + mm(w_lo[jj], back)

    for jj in range(nz - 1):
        part = partial_sum(jj)
        if jj >= 2:
            ring_copy(jj - 2).wait_recv()
            part = part + ring_in[jj - 2].astype(F32)
        ring_out[jj] = part.astype(BF16)
        ring_copy(jj).start()
    moe = partial_sum(nz - 1)
    for jj in (nz - 3, nz - 2):
        ring_copy(jj).wait_recv()
        moe = moe + ring_in[jj].astype(F32)
    out[...] = (resid[...] + moe).astype(BF16)

    for k in (1, 2, 3):
        ag_copy(k).wait_send()
        rs_copy(k).wait_send()
        st_copy(k).wait_send()
        rb_copy(k).wait_send()
    for a in range(3):
        for i in range(2):
            @pl.when(2 * core + i != my)
            def _():
                w_remote(a, i, pl.ds(0, ff)).wait_send()

    @pl.when(primary)
    def _():
        for a in range(3):
            for j in range(4):
                w_forward(a, j).wait_send()

    d_wait(send1.at[pl.ds(0, (nx * nz - 1) * BLK)], d1_s)
    for jj in range(nz):
        d_wait(recv2.at[0, pl.ds(0, (nx * 4 - 1) * BLK)], d2_s)
    for jj in range(nz - 1):
        ring_copy(jj).wait_send()
    d_wait(ids_all.at[pl.ds(0, nz - 1)], id_s.at[0])
    d_wait(rw_all.at[pl.ds(0, nz - 1)], id_s.at[1])


def perm_tables():
    index = np.arange(4 * BLK)
    l, b, c = index // BLK, (index % BLK) // CAP, index % CAP
    table = np.zeros((4 * BLK, 4 * BLK), np.float32)
    table[index, b * BLK + l * CAP + c] = 1.0
    return table, table.T.copy()


def body(
    nx, nz,
    hidden_in, norm_in_gain, q_weight, k_weight, v_weight, q_gain, k_gain, o_weight,
    key_pages, value_pages, page_table, cache_len, norm_post_gain, expert_ids, route_weights,
    gate_weight, up_weight, down_weight,
):
    n_chip = nx * nz
    width = hidden_in.shape[1]
    model = norm_in_gain.shape[0]
    ff = gate_weight.shape[2]
    half = np.arange(64, dtype=np.float64)
    freq = np.power(ROPE_BASE, -2.0 * half / 128.0)
    slots = np.arange(nx * 4 * CAP)
    home_r = slots // (4 * CAP) * nz * 4 + slots // CAP % 4
    line = np.arange(n_chip * CAP) // CAP
    home = ((line % nx) * nz + line // nx) * 4
    home_t = np.broadcast_to(home[:, None], (n_chip * CAP, TOK))
    slot_t = np.broadcast_to((np.arange(n_chip * CAP) % CAP)[:, None], (n_chip * CAP, TOK))
    p1, p2 = perm_tables()
    small = [
        hidden_in, norm_in_gain[None, :], q_gain[None, :], k_gain[None, :],
        norm_post_gain.reshape(4, 1, width), jnp.asarray(freq[None, :], F32), page_table,
        expert_ids.T, route_weights.T,
        jnp.asarray(home_t, jnp.int32), jnp.asarray(slot_t, F32),
        jnp.asarray(home_r[None, :], jnp.int32), jnp.asarray((slots % CAP)[None, :], F32), jnp.asarray(p1, BF16), jnp.asarray(p2, BF16),
    ]
    cache = POOL * PAGE
    large = [
        q_weight, k_weight, v_weight, o_weight,
        key_pages.reshape(cache, 128), value_pages.reshape(cache, 128),
        jnp.swapaxes(gate_weight, 1, 2), jnp.swapaxes(up_weight, 1, 2), down_weight,
    ]
    vmem = lambda shape, dtype=BF16: pltpu.VMEM(shape, dtype)
    dma = pltpu.SemaphoreType.DMA
    rows = n_chip * CAP
    return pl.pallas_call(
        functools.partial(layer_kernel, nx, nz),
        out_shape=jax.ShapeDtypeStruct((TOK, width), BF16),
        in_specs=[pl.BlockSpec(memory_space=pltpu.SMEM)]
        + [pl.BlockSpec(memory_space=pltpu.VMEM)] * len(small)
        + [pl.BlockSpec(memory_space=pl.ANY)] * len(large),
        out_specs=pl.BlockSpec(memory_space=pltpu.VMEM),
        scratch_shapes=[
            vmem((POOL, PAGE), jnp.int32), vmem((TOK, 128), F32), vmem((TOK, 128), F32),
            vmem((4, TOK, width)), vmem((TOK, model)),
            vmem(q_weight.shape), vmem(k_weight.shape), vmem(v_weight.shape), vmem(o_weight.shape),
            vmem((cache, 128)), vmem((cache, 128)),
            vmem((4 * TOK, 128)), vmem((TOK, 128)), vmem((TOK, 128)), vmem((TOK, 512)),
            vmem((4, TOK, width)), vmem((3, TOK, width)),
            vmem((8, TOK), F32), vmem((3, 8, TOK), F32),
            vmem((4, TOK, width)), vmem((TOK, width), F32),
            vmem((rows, TOK)), vmem((nz, TOK, nx * 4 * CAP)), vmem((nz, TOK, nx * 4 * CAP)),
            vmem((n_chip * BLK, width)), vmem((n_chip * BLK, width)),
            vmem((nz, 8, TOK), jnp.int32), vmem((nz, 8, TOK), F32), vmem((rows, model)),
            vmem((4, ff, model)), vmem((4, ff, model)), vmem((4, ff, model)),
            vmem((4, rows, ff)), vmem((rows, model), F32),
            vmem((4, n_chip * BLK, 128)), vmem((nz, nx * 4 * BLK, 128)),
            vmem((nz - 1, TOK, width)), vmem((nz - 1, TOK, width)),
            dma((6,)), dma((3,)), dma((3,)), dma((3,)), dma((3,)), dma((3,)), dma((3,)),
            dma((3,)), dma((3,)), dma, dma((nz,)), dma, dma((nz,)), dma((3, 2)), dma((3, 4)), dma((3, 4)),
            dma((2,)), dma((2,)), dma((nz - 1,)), dma((nz - 1,)),
        ],
        compiler_params=pltpu.CompilerParams(
            collective_id=0, has_side_effects=True, vmem_limit_bytes=62 * 1024 * 1024
        ),
    )(cache_len, *small, *large)


def solution(mesh):
    nx = 4
    nz = mesh.shape["req"] // (2 * nx)
    return jax.shard_map(
        functools.partial(body, nx, nz),
        mesh=mesh,
        in_specs=(
            P("req", "tp"), P(), P(None, "tp"), P(None, "tp"), P(None, "tp"), P(), P(),
            P("tp", None), P("tp", "req", None, None), P("tp", "req", None, None),
            P("req", None), P("req"), P(), P("req", None), P("req", None),
            P("req", None, "tp"), P("req", None, "tp"), P("req", "tp", None),
        ),
        out_specs=P("req", "tp"),
        check_vma=False,
    )
```

```python
import functools
import math

import jax
import jax.numpy as jnp
import numpy as np
from jax import lax
from jax.experimental import pallas as pl
from jax.experimental.pallas import tpu as pltpu
from jax.sharding import PartitionSpec as P

PAGE = 128
MAXPG = 32
PRE = 120
TOK = 128
REQS_DEV = 9
POOL = 48
CAP = 12
NORM_EPS = 1e-06
ROPE_BASE = 1000000.0

MESH = pl.DeviceIdType.MESH
F32 = jnp.float32
BF16 = jnp.bfloat16
BLK = 48
CHUNK = 512
PIECES = 6
EARLY = 3


def mm(a, b):
    return jnp.dot(a, b, preferred_element_type=F32)


def mm_t(a, b):
    return lax.dot_general(a, b, (((1,), (1,)), ((), ())), preferred_element_type=F32)


def iota(shape, dim):
    return lax.broadcasted_iota(jnp.int32, shape, dim)


def layer_kernel(
    nx, nz,
    lens, hid, gin, qgain, kgain, gpost, freq, table, ids_t, rw_t,
    home_t, slot_t, home_r, slot_r, perm1, perm2,
    qw, kw, vw, ow, kp, vp, wg_in, wu_in, wd_in,
    out,
    owner, cos_t, sin_t, xbuf, nbuf, qw_v, kw_v, vw_v, ow_v, kc, vc, q2, kn, vn, abuf,
    rs_send, rs_recv, st_send, st_recv, rbuf, resid, s_mat, w_hi, w_lo,
    send1, recv1, ids_all, rw_all, xe, wg, wu, wd, hbuf, ye, send2, recv2, ring_out, ring_in,
    loc_s, ag_s, ag_r, rs_s, rs_r, st_s, st_r, rb_s, rb_r, d1_s, d1_r, d2_s, d2_r, w_s, w_r, f_s, id_s, id_r, rg_s, rg_r,
):
    me_r = lax.axis_index("req")
    my = lax.axis_index("tp")
    core = lax.rem(me_r, 2)
    chip = me_r // 2
    cx = chip // nz
    cz = lax.rem(chip, nz)
    n_chip = nx * nz
    src_slot = cz * nx + cx
    ff = wd.shape[1]

    def peer(k):
        return lax.rem(my + k, 4)

    barrier = pltpu.get_barrier_semaphore()

    def greet(device):
        pl.semaphore_signal(barrier, inc=1, device_id=device, device_id_type=MESH)

    for k in range(1, n_chip):
        greet({"req": lax.rem(chip + k, n_chip) * 2 + core})
    for dx in range(nx):
        for k in (1, 2, 3):
            greet({"req": (lax.rem(cx + dx, nx) * nz + cz) * 2 + core, "tp": peer(k)})
    sibling = {"req": chip * 2 + 1 - core, "tp": my}
    greet(sibling)
    n_peers = n_chip + 3 * nx

    loads = [
        pltpu.make_async_copy(s, d, loc_s.at[i])
        for i, (s, d) in enumerate(
            [(qw, qw_v), (kw, kw_v), (vw, vw_v), (kp, kc), (vp, vc), (ow, ow_v)]
        )
    ]
    for load in loads:
        load.start()
    xbuf[my] = hid[...]

    lane = iota((TOK, TOK), 1)
    sub = iota((TOK, TOK), 0)

    def routes(group_ids, group_rw):
        named = jnp.zeros((TOK, TOK), F32)
        dense = jnp.zeros((TOK, TOK), F32)
        for k in range(8):
            hit = (group_ids[k : k + 1, :] == sub).astype(F32)
            named = named + hit
            dense = dense + hit * group_rw[k : k + 1, :]
        rank = mm(named.astype(BF16), (sub < lane).astype(BF16))
        return jnp.where(named > 0, rank, -1.0), dense

    homes = (home_t[...] + my == iota(home_t.shape, 1)).astype(BF16)
    rank_t, _ = routes(ids_t[...], rw_t[...])
    s_mat[...] = (mm(homes, rank_t.astype(BF16)) == slot_t[...]).astype(BF16)
    ids_all[cz] = ids_t[...]
    rw_all[cz] = rw_t[...]

    page = iota((POOL, MAXPG), 0)
    entry = iota((POOL, MAXPG), 1)
    own_sum = jnp.zeros((POOL, MAXPG), jnp.int32)
    start_sum = jnp.zeros((POOL, MAXPG), jnp.int32)
    len_sum = jnp.zeros((POOL, MAXPG), jnp.int32)
    tok_col = iota((TOK, 64), 0)
    tok_req = jnp.where(tok_col < PRE, 0, tok_col - PRE + 1)
    position = jnp.where(tok_col < PRE, tok_col, 0)
    for r in range(REQS_DEV):
        length = lens[r]
        match = (table[r : r + 1, :] == page) & (entry * PAGE < length)
        own_sum = own_sum + jnp.where(match, r + 1, 0)
        start_sum = start_sum + jnp.where(match, entry * PAGE, 0)
        len_sum = len_sum + jnp.where(match, length, 0)
        position = position + jnp.where(tok_req == r, length, 0)

    def lane_sum(v):
        return jnp.sum(v.astype(F32), axis=1, keepdims=True).astype(jnp.int32)

    slot_pos = lane_sum(start_sum) + iota((POOL, PAGE), 1)
    own_col = lane_sum(own_sum)
    owner[...] = jnp.where((own_col > 0) & (slot_pos < lane_sum(len_sum)), own_col - 1, -1)
    angle = position.astype(F32) * freq[...]
    cosine, sine = jnp.cos(angle), jnp.sin(angle)
    cos_t[...] = jnp.concatenate([cosine, cosine], axis=1)
    sin_t[...] = jnp.concatenate([-sine, sine], axis=1)

    pl.semaphore_wait(barrier, n_peers)

    def ag_copy(k):
        return pltpu.make_async_remote_copy(
            src_ref=hid, dst_ref=xbuf.at[my], send_sem=ag_s.at[k - 1], recv_sem=ag_r.at[k - 1],
            device_id={"tp": peer(k)}, device_id_type=MESH,
        )

    for k in (1, 3, 2):
        ag_copy(k).start()

    def table_copies(k):
        device = {"req": (cx * nz + lax.rem(cz + k, nz)) * 2 + core}
        return [
            pltpu.make_async_remote_copy(
                src_ref=src, dst_ref=dst.at[cz], send_sem=id_s.at[i], recv_sem=id_r.at[i],
                device_id=device, device_id_type=MESH,
            )
            for i, (src, dst) in enumerate([(ids_t, ids_all), (rw_t, rw_all)])
        ]

    for k in range(1, nz):
        for copy in table_copies(k):
            copy.start()

    w_pairs = ((wg_in, wg), (wu_in, wu), (wd_in, wd))

    piece = ff // PIECES

    def slot(a, t):
        return t if a == 2 else 0

    def w_remote(a, i, t, rows):
        return pltpu.make_async_remote_copy(
            src_ref=w_pairs[a][0].at[i, rows], dst_ref=w_pairs[a][1].at[my, rows],
            send_sem=w_s.at[a, i], recv_sem=w_r.at[a, my, slot(a, t)],
            device_id={"tp": 2 * core + i}, device_id_type=MESH,
        )

    def w_start(a, t):
        rows = pl.ds(t * piece, piece)
        for i in range(2):
            @pl.when(2 * core + i != my)
            def _():
                w_remote(a, i, t, rows).start()

            @pl.when(2 * core + i == my)
            def _():
                pltpu.make_async_copy(
                    w_pairs[a][0].at[i, rows],
                    w_pairs[a][1].at[my, rows],
                    w_r.at[a, my, slot(a, t)],
                ).start()

    def w_part(a, j, t):
        rows = pl.ds(t * piece, piece) if a == 2 else pl.ds(0, ff)
        return w_pairs[a][1].at[j, rows]

    def w_forward(a, j, t):
        ref = w_part(a, j, t)
        return pltpu.make_async_remote_copy(
            src_ref=ref, dst_ref=ref, send_sem=f_s.at[a, j], recv_sem=w_r.at[a, j, t],
            device_id=sibling, device_id_type=MESH,
        )

    def w_wait(a, j, t):
        ref = w_part(a, j, t)
        pltpu.make_async_copy(ref, ref, w_r.at[a, j, t]).wait()

    primary = core == my // 2

    def w_pass_on(a, t, offs=(0, 1, 3, 2)):
        @pl.when(primary)
        def _():
            for off in offs:
                w_wait(a, peer(off), t)
                w_forward(a, peer(off), t).start()

    for t in range(EARLY):
        w_start(0, t)

    for k in (1, 3, 2):
        ag_copy(k).wait_recv()
    x_all = jnp.concatenate([xbuf[j].astype(F32) for j in range(4)], axis=1)
    mean_sq = jnp.mean(x_all * x_all, axis=-1, keepdims=True)
    nbuf[...] = (x_all * lax.rsqrt(mean_sq + NORM_EPS) * gin[...]).astype(BF16)
    for load in loads[:3]:
        load.wait()

    def head_norm(v, gain):
        ms = jnp.mean(v * v, axis=-1, keepdims=True)
        v = v * lax.rsqrt(ms + NORM_EPS) * gain
        return (v * cos_t[...] + pltpu.roll(v, 64, 1) * sin_t[...]).astype(BF16)

    score_scale = math.log2(math.e) / math.sqrt(128)
    q_lin = mm(nbuf[...], qw_v[...])
    for g in range(4):
        q2[g * TOK : (g + 1) * TOK, :] = head_norm(
            q_lin[:, g * 128 : (g + 1) * 128], qgain[...] * score_scale
        )
    kn[...] = head_norm(mm(nbuf[...], kw_v[...]), kgain[...])
    vn[...] = mm(nbuf[...], vw_v[...]).astype(BF16)

    n_q = 4 * TOK
    row_tok = lax.rem(iota((n_q, 1), 0), TOK)
    row_req = jnp.where(row_tok < PRE, 0, row_tok - PRE + 1)
    key_tok = iota((n_q, TOK), 1)
    new_mask = (key_tok == row_tok) | ((row_tok < PRE) & (key_tok <= row_tok))
    sc = jnp.where(new_mask, mm_t(q2[...], kn[...]), -1e30)
    m0 = jnp.max(sc, axis=-1, keepdims=True)
    pr = jnp.exp2(sc - m0)
    l0 = jnp.sum(pr, axis=-1, keepdims=True)
    acc0 = mm(pr.astype(BF16), vn[...])
    for load in loads[3:5]:
        load.wait()

    def attend_chunk(j, carry):
        m, l, acc = carry
        at = pl.multiple_of(j * CHUNK, CHUNK)
        s = mm_t(q2[...], kc[pl.ds(at, CHUNK), :])
        own = jnp.concatenate(
            [owner[pl.ds(j * (CHUNK // PAGE) + i, 1), :] for i in range(CHUNK // PAGE)], axis=1
        )
        s = jnp.where(own == row_req, s, -1e30)
        m_new = jnp.maximum(m, jnp.max(s, axis=-1, keepdims=True))
        scale = jnp.exp2(m - m_new)
        p = jnp.exp2(s - m_new)
        l = l * scale + jnp.sum(p, axis=-1, keepdims=True)
        acc = acc * scale + mm(p.astype(BF16), vc[pl.ds(at, CHUNK), :])
        return m_new, l, acc

    _, l_all, acc_all = lax.fori_loop(
        0, POOL * PAGE // CHUNK, attend_chunk, (m0, l0, acc0), unroll=4
    )
    att = (acc_all / l_all).astype(BF16)
    for g in range(4):
        abuf[:, g * 128 : (g + 1) * 128] = att[g * TOK : (g + 1) * TOK, :]
    loads[5].wait()
    for j in range(4):
        rs_send[j] = mm(abuf[...], ow_v[:, j * 512 : (j + 1) * 512]).astype(BF16)

    def rs_copy(k):
        return pltpu.make_async_remote_copy(
            src_ref=rs_send.at[peer(k)], dst_ref=rs_recv.at[k - 1],
            send_sem=rs_s.at[k - 1], recv_sem=rs_r.at[k - 1],
            device_id={"tp": peer(k)}, device_id_type=MESH,
        )

    for k in (1, 3, 2):
        rs_copy(k).start()
    total = hid[...].astype(F32) + rs_send[my].astype(F32)
    for k in (1, 3, 2):
        rs_copy(k).wait_recv()
        total = total + rs_recv[k - 1].astype(F32)
    resid[...] = total
    rbuf[my] = total.astype(BF16)
    col = jnp.sum(total * total, axis=-1, keepdims=True)
    diag = sub == lane
    row = jnp.sum(jnp.where(diag, col, 0.0), axis=0, keepdims=True)
    st_send[...] = jnp.broadcast_to(row, (8, TOK))

    def rb_copy(k):
        return pltpu.make_async_remote_copy(
            src_ref=rbuf.at[my], dst_ref=rbuf.at[my],
            send_sem=rb_s.at[k - 1], recv_sem=rb_r.at[k - 1],
            device_id={"tp": peer(k)}, device_id_type=MESH,
        )

    def st_copy(k):
        return pltpu.make_async_remote_copy(
            src_ref=st_send, dst_ref=st_recv.at[k - 1],
            send_sem=st_s.at[k - 1], recv_sem=st_r.at[k - 1],
            device_id={"tp": peer(k)}, device_id_type=MESH,
        )

    for k in (1, 3, 2):
        st_copy(k).start()
        rb_copy(k).start()
    for t in range(EARLY, PIECES):
        w_start(0, t)
    for a in (1, 2):
        for t in range(PIECES):
            w_start(a, t)
    for k in (1, 3, 2):
        st_copy(k).wait_recv()
        rb_copy(k).wait_recv()
    row = st_send[0:1, :] + st_recv[0, 0:1, :] + st_recv[1, 0:1, :] + st_recv[2, 0:1, :]
    col = jnp.sum(jnp.where(diag, row, 0.0), axis=-1, keepdims=True)
    row_scale = lax.rsqrt(col * (1.0 / 2048.0) + NORM_EPS)
    for j in range(4):
        nbuf[:, j * 512 : (j + 1) * 512] = (
            rbuf[j].astype(F32) * row_scale * gpost[j]
        ).astype(BF16)

    def dz_of(jj):
        return lax.rem(nz // 2 + ((jj + 1) // 2) * (2 * lax.rem(jj, 2) - 1) + nz, nz)

    def plane(jj):
        return lax.rem(cz + dz_of(jj), nz)

    def chip_at(jj, dx):
        return lax.rem(cx + dx, nx), plane(jj)

    def d1_copy(jj, dx, local=False):
        gx, gz = chip_at(jj, dx)
        src = send1.at[pl.ds(pl.multiple_of((gz * nx + gx) * BLK, 16), BLK)]
        dst = recv1.at[pl.ds(pl.multiple_of(src_slot * BLK, 16), BLK)]
        if local:
            return pltpu.make_async_copy(src, dst, d1_r.at[jj])
        return pltpu.make_async_remote_copy(
            src_ref=src, dst_ref=dst, send_sem=d1_s, recv_sem=d1_r.at[jj],
            device_id={"req": (gx * nz + gz) * 2 + core}, device_id_type=MESH,
        )

    def d2_copy(jj, dx, k, local=False):
        gx, gz = chip_at(jj, dx)
        src = send2.at[peer(k), pl.ds(pl.multiple_of((gz * nx + gx) * BLK, 16), BLK)]
        dst = recv2.at[jj, pl.ds(pl.multiple_of((cx * 4 + my) * BLK, 16), BLK)]
        if local:
            return pltpu.make_async_copy(src, dst, d2_r.at[jj])
        return pltpu.make_async_remote_copy(
            src_ref=src, dst_ref=dst, send_sem=d2_s, recv_sem=d2_r.at[jj],
            device_id={"req": (gx * nz + cz) * 2 + core, "tp": peer(k)}, device_id_type=MESH,
        )

    def send_back(jj):
        for dx in (2, 1, 3, 0):
            for k in (2, 1, 3, 0):
                d2_copy(jj, dx, k, local=dx == 0 and k == 0).start()

    def send_line(jj, last=False):
        for dx in range(nx):
            d1_copy(jj, dx, local=last and dx == 0).start()

    def build(jj):
        gz = plane(jj)
        z = mm(s_mat[pl.ds(pl.multiple_of(gz * BLK, 16), BLK), :], nbuf[...]).astype(BF16)
        parts = jnp.concatenate([z[:, i * 512 : (i + 1) * 512] for i in range(4)], axis=0)
        at = pl.multiple_of(gz * nx * BLK, 16)
        send1[pl.ds(at, nx * BLK), :] = mm(perm2[...], parts).astype(BF16)

    build(0)

    def build_step(jj, carry):
        build(jj)
        send_line(jj - 1)
        return carry

    lax.fori_loop(1, nz, build_step, 0)
    send_line(nz - 1, last=True)

    def d_wait(ref, sem):
        pltpu.make_async_copy(ref, ref, sem).wait()

    d_wait(ids_all.at[pl.ds(0, nz - 1)], id_r.at[0])
    d_wait(rw_all.at[pl.ds(0, nz - 1)], id_r.at[1])
    spread = (home_r[...] + 4 * cz == iota((TOK, home_r.shape[1]), 0)).astype(BF16)

    def weigh(jj, carry):
        gz = plane(jj)
        rank_t, dense_t = routes(ids_all[gz], rw_all[gz])
        chosen = mm(rank_t.T.astype(BF16), spread) == slot_r[...]
        dense_w = dense_t.T
        dw_hi = dense_w.astype(BF16)
        dw_lo = (dense_w - dw_hi.astype(F32)).astype(BF16)
        w_hi[jj] = jnp.where(chosen, mm(dw_hi, spread), 0.0).astype(BF16)
        w_lo[jj] = jnp.where(chosen, mm(dw_lo, spread), 0.0).astype(BF16)
        return carry

    lax.fori_loop(0, nz, weigh, 0)

    w_pass_on(0, 0)
    w_pass_on(1, 0)
    for t in range(PIECES):
        w_pass_on(2, t, (0,))

    def w_wait_all(a):
        @pl.when(jnp.logical_not(primary))
        def _():
            for j in range(4):
                for t in range(PIECES if a == 2 else 1):
                    w_wait(a, j, t)

    def unpack(jj, carry):
        gz = plane(jj)
        o = mm(perm1[...], recv1[pl.ds(pl.multiple_of(gz * nx * BLK, 16), nx * BLK), :]).astype(BF16)
        to = pl.multiple_of(jj * BLK, 16)
        for i in range(4):
            xe[pl.ds(to, BLK), i * 512 : (i + 1) * 512] = o[i * BLK : (i + 1) * BLK, :]
        return carry

    steps = [(nz // 2 + (j + 1) // 2 * (2 * (j % 2) - 1)) % nz for j in range(nz)]
    from_sem = [steps.index((nz - d) % nz) for d in steps]
    half_rows = n_chip * CAP // 2

    for half in range(2):
        first = half * (nz // 2)
        for jj in range(first, first + nz // 2):
            d_wait(recv1.at[pl.ds(0, nx * BLK)], d1_r.at[from_sem[jj]])
        if half == 1:
            for t in range(PIECES // 3, PIECES - 2):
                w_pass_on(2, t, (1, 3, 2))
        lax.fori_loop(first, first + nz // 2, unpack, 0)
        if half == 0:
            w_wait_all(0)
            w_wait_all(1)
        rows = pl.ds(half * half_rows, half_rows)

        def act_step(j, carry):
            x = xe[rows, :]
            gate = mm_t(x, wg[j])
            up = mm_t(x, wu[j])
            hbuf[j, rows, :] = (gate / (1.0 + jnp.exp(-gate)) * up).astype(BF16)
            return carry

        if half == 0:
            lax.fori_loop(0, 4, act_step, 0)
            for t in range(PIECES // 3):
                w_pass_on(2, t, (1, 3, 2))
        else:
            for step in range(2):
                act_step(step, 0)
                w_pass_on(2, PIECES - 2 + step, (1, 3, 2))
            lax.fori_loop(2, 4, act_step, 0)
    w_wait_all(2)

    def pack(jj):
        gz = plane(jj)
        rows = pl.ds(pl.multiple_of(jj * BLK, 16), BLK)
        parts = []
        for i in range(4):
            parts.append(
                jnp.concatenate(
                    [ye[rows, (q * 4 + i) * 128 : (q * 4 + i + 1) * 128] for q in range(4)], axis=1
                ).astype(BF16)
            )
        o = mm(perm2[...], jnp.concatenate(parts, axis=0)).astype(BF16)
        at = pl.multiple_of(gz * nx * BLK, 16)
        for q in range(4):
            send2[q, pl.ds(at, nx * BLK), :] = o[:, q * 128 : (q + 1) * 128]

    for half in range(2):
        rows = pl.ds(half * half_rows, half_rows)
        ye[rows, :] = mm(hbuf[0, rows, :], wd[0])

        def down_step(j, carry):
            ye[rows, :] += mm(hbuf[j, rows, :], wd[j])
            return carry

        lax.fori_loop(1, 4, down_step, 0)
        first = half * (nz // 2)
        pack(first)

        def pack_step(jj, carry):
            pack(jj)
            send_back(jj - 1)
            return carry

        lax.fori_loop(first + 1, first + nz // 2, pack_step, 0)
        send_back(first + nz // 2 - 1)

    def ring_copy(jj):
        step = 1 if jj % 2 == 0 else nz - 1
        return pltpu.make_async_remote_copy(
            src_ref=ring_out.at[jj], dst_ref=ring_in.at[jj],
            send_sem=rg_s.at[jj], recv_sem=rg_r.at[jj],
            device_id={"req": (cx * nz + lax.rem(cz + step, nz)) * 2 + core}, device_id_type=MESH,
        )

    def partial_sum(jj):
        d_wait(recv2.at[jj], d2_r.at[jj])
        x = jnp.concatenate(
            [recv2[jj, i * 4 * BLK : (i + 1) * 4 * BLK, :] for i in range(nx)], axis=1
        )
        o = mm(perm1[...], x).astype(BF16)
        rows = [
            jnp.concatenate(
                [o[q * BLK : (q + 1) * BLK, i * 128 : (i + 1) * 128] for q in range(4)], axis=1
            )
            for i in range(nx)
        ]
        back = jnp.concatenate(rows, axis=0)
        return mm(w_hi[jj], back) + mm(w_lo[jj], back)

    for jj in range(nz - 1):
        part = partial_sum(jj)
        if jj >= 2:
            ring_copy(jj - 2).wait_recv()
            part = part + ring_in[jj - 2].astype(F32)
        ring_out[jj] = part.astype(BF16)
        ring_copy(jj).start()
    moe = partial_sum(nz - 1)
    for jj in (nz - 3, nz - 2):
        ring_copy(jj).wait_recv()
        moe = moe + ring_in[jj].astype(F32)
    out[...] = (resid[...] + moe).astype(BF16)

    for k in (1, 2, 3):
        ag_copy(k).wait_send()
        rs_copy(k).wait_send()
        st_copy(k).wait_send()
        rb_copy(k).wait_send()
    for a in range(3):
        for i in range(2):
            @pl.when(2 * core + i != my)
            def _():
                w_remote(a, i, 0, pl.ds(0, ff)).wait_send()

    @pl.when(primary)
    def _():
        for a in range(3):
            for j in range(4):
                for t in range(PIECES if a == 2 else 1):
                    w_forward(a, j, t).wait_send()

    d_wait(send1.at[pl.ds(0, (nx * nz - 1) * BLK)], d1_s)
    for jj in range(nz):
        d_wait(recv2.at[0, pl.ds(0, (nx * 4 - 1) * BLK)], d2_s)
    for jj in range(nz - 1):
        ring_copy(jj).wait_send()
    d_wait(ids_all.at[pl.ds(0, nz - 1)], id_s.at[0])
    d_wait(rw_all.at[pl.ds(0, nz - 1)], id_s.at[1])


def perm_tables():
    index = np.arange(4 * BLK)
    l, b, c = index // BLK, (index % BLK) // CAP, index % CAP
    table = np.zeros((4 * BLK, 4 * BLK), np.float32)
    table[index, b * BLK + l * CAP + c] = 1.0
    return table, table.T.copy()


def body(
    nx, nz,
    hidden_in, norm_in_gain, q_weight, k_weight, v_weight, q_gain, k_gain, o_weight,
    key_pages, value_pages, page_table, cache_len, norm_post_gain, expert_ids, route_weights,
    gate_weight, up_weight, down_weight,
):
    n_chip = nx * nz
    width = hidden_in.shape[1]
    model = norm_in_gain.shape[0]
    ff = gate_weight.shape[2]
    half = np.arange(64, dtype=np.float64)
    freq = np.power(ROPE_BASE, -2.0 * half / 128.0)
    slots = np.arange(nx * 4 * CAP)
    home_r = slots // (4 * CAP) * nz * 4 + slots // CAP % 4
    line = np.arange(n_chip * CAP) // CAP
    home = ((line % nx) * nz + line // nx) * 4
    home_t = np.broadcast_to(home[:, None], (n_chip * CAP, TOK))
    slot_t = np.broadcast_to((np.arange(n_chip * CAP) % CAP)[:, None], (n_chip * CAP, TOK))
    p1, p2 = perm_tables()
    small = [
        hidden_in, norm_in_gain[None, :], q_gain[None, :], k_gain[None, :],
        norm_post_gain.reshape(4, 1, width), jnp.asarray(freq[None, :], F32), page_table,
        expert_ids.T, route_weights.T,
        jnp.asarray(home_t, jnp.int32), jnp.asarray(slot_t, F32),
        jnp.asarray(home_r[None, :], jnp.int32), jnp.asarray((slots % CAP)[None, :], F32), jnp.asarray(p1, BF16), jnp.asarray(p2, BF16),
    ]
    cache = POOL * PAGE
    large = [
        q_weight, k_weight, v_weight, o_weight,
        key_pages.reshape(cache, 128), value_pages.reshape(cache, 128),
        jnp.swapaxes(gate_weight, 1, 2), jnp.swapaxes(up_weight, 1, 2), down_weight,
    ]
    vmem = lambda shape, dtype=BF16: pltpu.VMEM(shape, dtype)
    dma = pltpu.SemaphoreType.DMA
    rows = n_chip * CAP
    return pl.pallas_call(
        functools.partial(layer_kernel, nx, nz),
        out_shape=jax.ShapeDtypeStruct((TOK, width), BF16),
        in_specs=[pl.BlockSpec(memory_space=pltpu.SMEM)]
        + [pl.BlockSpec(memory_space=pltpu.VMEM)] * len(small)
        + [pl.BlockSpec(memory_space=pl.ANY)] * len(large),
        out_specs=pl.BlockSpec(memory_space=pltpu.VMEM),
        scratch_shapes=[
            vmem((POOL, PAGE), jnp.int32), vmem((TOK, 128), F32), vmem((TOK, 128), F32),
            vmem((4, TOK, width)), vmem((TOK, model)),
            vmem(q_weight.shape), vmem(k_weight.shape), vmem(v_weight.shape), vmem(o_weight.shape),
            vmem((cache, 128)), vmem((cache, 128)),
            vmem((4 * TOK, 128)), vmem((TOK, 128)), vmem((TOK, 128)), vmem((TOK, 512)),
            vmem((4, TOK, width)), vmem((3, TOK, width)),
            vmem((8, TOK), F32), vmem((3, 8, TOK), F32),
            vmem((4, TOK, width)), vmem((TOK, width), F32),
            vmem((rows, TOK)), vmem((nz, TOK, nx * 4 * CAP)), vmem((nz, TOK, nx * 4 * CAP)),
            vmem((n_chip * BLK, width)), vmem((n_chip * BLK, width)),
            vmem((nz, 8, TOK), jnp.int32), vmem((nz, 8, TOK), F32), vmem((rows, model)),
            vmem((4, ff, model)), vmem((4, ff, model)), vmem((4, ff, model)),
            vmem((4, rows, ff)), vmem((rows, model), F32),
            vmem((4, n_chip * BLK, 128)), vmem((nz, nx * 4 * BLK, 128)),
            vmem((nz - 1, TOK, width)), vmem((nz - 1, TOK, width)),
            dma((6,)), dma((3,)), dma((3,)), dma((3,)), dma((3,)), dma((3,)), dma((3,)),
            dma((3,)), dma((3,)), dma, dma((nz,)), dma, dma((nz,)), dma((3, 2)), dma((3, 4, PIECES)), dma((3, 4)),
            dma((2,)), dma((2,)), dma((nz - 1,)), dma((nz - 1,)),
        ],
        compiler_params=pltpu.CompilerParams(
            collective_id=0, has_side_effects=True, vmem_limit_bytes=62 * 1024 * 1024
        ),
    )(cache_len, *small, *large)


def solution(mesh):
    nx = 4
    nz = mesh.shape["req"] // (2 * nx)
    return jax.shard_map(
        functools.partial(body, nx, nz),
        mesh=mesh,
        in_specs=(
            P("req", "tp"), P(), P(None, "tp"), P(None, "tp"), P(None, "tp"), P(), P(),
            P("tp", None), P("tp", "req", None, None), P("tp", "req", None, None),
            P("req", None), P("req"), P(), P("req", None), P("req", None),
            P("req", None, "tp"), P("req", None, "tp"), P("req", "tp", None),
        ),
        out_specs=P("req", "tp"),
        check_vma=False,
    )
```
